32 devices in a mesh: groups: 2 (over x), tier: 16 (over z, y, core).
Axes of the slice: x: 2, y: 2, z: 4, core: 2. Of those that a mesh axis runs over, the one named last changes fastest.
Arguments:
- rho: float32 [256, 2, 256, 256], P(('groups', 'tier')), parts along dimension 0, may hold values from -6 to 6
- hamiltonian: float32 [256, 256], replicated, may hold values from -0.375 to 0.375
- couplings: float32 [4, 256, 256], replicated, may hold values from -0.375 to 0.375
- bath_coef: float32 [8, 2], P('groups'), parts along dimension 0, may hold values from 0.3 to 1.5
- damping: float32 [256], P(('groups', 'tier')), parts along dimension 0, may hold values from 0.2 to 3
- match_edges: int32 [16, 4, 1, 5], P('tier'), may hold values from 0 to 7, as said below
- left_rows: int32 [16, 6, 5], replicated, may hold values from 0 to 127, as said below
- left_count: int32 [16], replicated, may hold values from 1 to 6, as said below
Outputs:
- rho_next: float32 [256, 2, 256, 256], P(('groups', 'tier')), parts along dimension 0
The draws below stay inside these ranges and needn't reach their ends.
There are 2 independent parts, one for each index of `groups`. The reference program is written for one: setup_inputs(seed, part) draws one part's arguments, and reference() takes and returns one part's arrays. A program takes and returns all parts, laid end to end along the dimension named above; an argument that names none is the same for every part. Nothing has to cross between parts.
Inputs may be any that keep to these rules, and one draw needn't show every extreme that they name: match_edges[b, c, j] = (target slot, partner slot, mode, lower flag 0 or 1, occupation 1 to 3); the row (b XOR 2^c, c, j) describes the same edge from the partner's side: its target slot is this row's partner slot and the reverse, same mode and occupation, opposite lower flag. left_rows[b, j] = (target slot, source matrix index, mode, lower flag 0 or 1, occupation 1 to 3); the source's block lies at cyclic block distance 1 to 4 from b, and the rows of one block name distinct source blocks. Only the first left_count[b] rows of block b are live; some block has exactly 6.
All inputs are finite; a program needn't handle non-finite values.
Results may differ from the reference program's by a relative error of at most 0.00005.
Values sent between devices are 32-bit elements; how exact they have to be, the bound alone decides.
A program may use at most 128 MiB of HBM per device.

```python
import math
import jax
import jax.numpy as jnp
from jax import lax

ORDER = 256
KMODES = 4
COLOURS = 4
PAIRS = 1
LEFT_CAP = 6
REACH = 4
MAT_DEV = 8
MATRICES = 128
N_TIER = 16


def match_tables(key):
    subkeys = jax.random.split(key, 4)
    blocks = jnp.arange(N_TIER, dtype=jnp.int32)
    slot_draw = jax.random.randint(subkeys[0], (COLOURS, N_TIER, PAIRS), 0, MAT_DEV)
    flag_draw = jax.random.randint(subkeys[1], (COLOURS, N_TIER, PAIRS), 0, 2)
    mode_draw = jax.random.randint(subkeys[2], (COLOURS, N_TIER, PAIRS), 0, KMODES)
    occ_draw = jax.random.randint(subkeys[3], (COLOURS, N_TIER, PAIRS), 1, 4)
    colour_rows = []
    for colour in range(COLOURS):
        stride = 2 ** colour
        upper_half = blocks // stride % 2
        partner = blocks + stride - 2 * stride * upper_half
        lowest = jnp.minimum(blocks, partner)
        own_slot = slot_draw[colour]
        their_slot = slot_draw[colour][partner]
        base_flag = flag_draw[colour][lowest]
        lower_flag = jnp.where(upper_half[:, None] == 0, base_flag, 1 - base_flag)
        mode_ids = mode_draw[colour][lowest]
        occupied = occ_draw[colour][lowest]
        colour_rows.append(jnp.stack([own_slot, their_slot, mode_ids, lower_flag, occupied], axis=-1))
    return jnp.stack(colour_rows, axis=1).astype(jnp.int32)


def draw_match_edges(key, part):
    return match_tables(jax.random.fold_in(key, 11))


def left_tables(key):
    subkeys = jax.random.split(key, 8)
    blocks = jnp.arange(N_TIER, dtype=jnp.int32)
    orders = jax.vmap(lambda sub: jax.random.permutation(sub, 2 * REACH))(jax.random.split(subkeys[0], N_TIER))
    picked = orders[:, :LEFT_CAP].astype(jnp.int32)
    offsets = jnp.where(picked < REACH, picked - REACH, picked - REACH + 1)
    src_block = (blocks[:, None] + offsets) % N_TIER
    src_slot = jax.random.randint(subkeys[1], (N_TIER, LEFT_CAP), 0, MAT_DEV)
    target_slot = jax.random.randint(subkeys[2], (N_TIER, LEFT_CAP), 0, MAT_DEV)
    mode_ids = jax.random.randint(subkeys[3], (N_TIER, LEFT_CAP), 0, KMODES)
    lower_flag = jax.random.randint(subkeys[4], (N_TIER, LEFT_CAP), 0, 2)
    occupied = jax.random.randint(subkeys[5], (N_TIER, LEFT_CAP), 1, 4)
    rows = jnp.stack([target_slot, src_block * MAT_DEV + src_slot, mode_ids, lower_flag, occupied], axis=-1)
    counts = jax.random.randint(subkeys[6], (N_TIER,), 1, LEFT_CAP // 2 + 1)
    busiest = jax.random.randint(subkeys[7], (), 0, N_TIER)
    counts = jnp.where(blocks == busiest, LEFT_CAP, counts)
    return (rows.astype(jnp.int32), counts.astype(jnp.int32))


def draw_left_rows(key, part):
    return left_tables(jax.random.fold_in(key, 23))[0]


def draw_left_count(key, part):
    return left_tables(jax.random.fold_in(key, 23))[1]


def levels(key, shape, shards, least, top_value):
    level, own = 1.0, jax.random.fold_in(key, 6)
    for dim, parts in shards:
        draws = jnp.exp(jax.random.uniform(jax.random.fold_in(own, dim), (parts,), jnp.float32, least / len(shards), top_value / len(shards)))
        level = level * jnp.repeat(draws, shape[dim] // parts).reshape([-1 if axis == dim else 1 for axis in range(len(shape))])
    return level


def gaussian(key, extent, scale, limit, cuts=(), kind=jnp.bfloat16):
    factor_of = levels(key, extent, cuts, -0.22, 0.18) if cuts else 1.0
    drawn = jax.random.normal(key, extent, jnp.float32) * scale * factor_of
    return jnp.minimum(jnp.maximum(drawn, -limit), limit).astype(kind)


def setup_inputs(seed: int = 0, part: int = 0) -> dict:
    seeds = jax.random.split(jax.random.key(seed), 9)
    part_splits = jax.random.split(jax.random.fold_in(seeds[8], part), 9)
    rho = gaussian(part_splits[0], (MATRICES, 2, ORDER, ORDER), 1.0, 6.0, ((0, 16),), jnp.float32)
    hamiltonian = gaussian(seeds[1], (ORDER, ORDER), ORDER ** -0.5, 0.375, (), jnp.float32)
    couplings = gaussian(seeds[2], (KMODES, ORDER, ORDER), ORDER ** -0.5, 0.375, (), jnp.float32)
    bath_coef = jnp.clip(jax.random.uniform(part_splits[3], (KMODES, 2), jnp.float32, 0.3, 1.5), 0.3, 1.5)
    damping = jnp.clip(jnp.exp(math.log(3.0) - 2.7080502 * jax.random.uniform(part_splits[4], (MATRICES,), jnp.float32) ** levels(part_splits[4], (MATRICES,), ((0, 16),), -0.2, 0.2)), 0.2, 3.0)
    match_edges = draw_match_edges(jax.random.fold_in(seeds[8], 71), part)
    left_rows = draw_left_rows(jax.random.fold_in(seeds[8], 71), part)
    left_count = draw_left_count(jax.random.fold_in(seeds[8], 71), part)
    return dict(rho=rho, hamiltonian=hamiltonian, couplings=couplings, bath_coef=bath_coef, damping=damping, match_edges=match_edges, left_rows=left_rows, left_count=left_count)


step_size = 0.1

def commute_hamiltonian(density, hamiltonian):
    left_side = jnp.einsum('ab,nxbc->nxac', hamiltonian, density, precision=lax.Precision.HIGHEST)
    right_side = jnp.einsum('nxab,bc->nxac', density, hamiltonian, precision=lax.Precision.HIGHEST)
    difference = left_side - right_side
    return jnp.stack([difference[:, 1], -difference[:, 0]], axis=1)

def edge_terms(sources, mode_ids, lower_flags, occupied, couplings, bath_coef):
    chosen = jnp.take(couplings, mode_ids, axis=0)
    left_prod = jnp.einsum('rab,rxbc->rxac', chosen, sources, precision=lax.Precision.HIGHEST)
    right_prod = jnp.einsum('rxab,rbc->rxac', sources, chosen, precision=lax.Precision.HIGHEST)
    is_lower = lower_flags == 1
    real_coef = jnp.where(is_lower, jnp.ones_like(bath_coef[:, 0])[0], jnp.take(bath_coef[:, 0], mode_ids))
    imag_coef = jnp.where(is_lower, jnp.zeros_like(bath_coef[:, 1])[0], jnp.take(bath_coef[:, 1], mode_ids))
    root_occ = jnp.sqrt(occupied.astype(jnp.float32))
    difference = left_prod - right_prod
    summed = left_prod + right_prod
    real_part = real_coef[:, None, None] * difference[:, 0] - imag_coef[:, None, None] * summed[:, 1]
    imag_part = real_coef[:, None, None] * difference[:, 1] + imag_coef[:, None, None] * summed[:, 0]
    return root_occ[:, None, None, None] * jnp.stack([imag_part, -real_part], axis=1)

def reference(rho, hamiltonian, couplings, bath_coef, damping, match_edges, left_rows, left_count):
    blocks = jnp.arange(N_TIER, dtype=jnp.int32)
    targets, anchors, mode_ids, lower_flags, occupied, weights = ([], [], [], [], [], [])
    for colour in range(COLOURS):
        stride = 2 ** colour
        upper_half = blocks // stride % 2
        partner = blocks + stride - 2 * stride * upper_half
        edge_table = match_edges[:, colour]
        targets.append((blocks[:, None] * MAT_DEV + edge_table[:, :, 0]).reshape(-1))
        anchors.append((partner[:, None] * MAT_DEV + edge_table[:, :, 1]).reshape(-1))
        mode_ids.append(edge_table[:, :, 2].reshape(-1))
        lower_flags.append(edge_table[:, :, 3].reshape(-1))
        occupied.append(edge_table[:, :, 4].reshape(-1))
        weights.append(jnp.ones((N_TIER * PAIRS,), jnp.float32))
    live_rows = jnp.arange(LEFT_CAP, dtype=jnp.int32)[None, :] < left_count[:, None]
    targets.append((blocks[:, None] * MAT_DEV + left_rows[:, :, 0]).reshape(-1))
    anchors.append(left_rows[:, :, 1].reshape(-1))
    mode_ids.append(left_rows[:, :, 2].reshape(-1))
    lower_flags.append(left_rows[:, :, 3].reshape(-1))
    occupied.append(left_rows[:, :, 4].reshape(-1))
    weights.append(live_rows.reshape(-1).astype(jnp.float32))
    targets = jnp.concatenate(targets).astype(jnp.int32)
    anchors = jnp.concatenate(anchors).astype(jnp.int32)
    mode_ids = jnp.concatenate(mode_ids).astype(jnp.int32)
    lower_flags = jnp.concatenate(lower_flags)
    occupied = jnp.concatenate(occupied)
    weights = jnp.concatenate(weights)

    def derivative(density):
        sources = jnp.take(density, anchors, axis=0)
        row_terms = edge_terms(sources, mode_ids, lower_flags, occupied, couplings, bath_coef)
        row_terms = row_terms * weights[:, None, None, None]
        coupled = jax.ops.segment_sum(row_terms, targets, num_segments=MATRICES)
        return commute_hamiltonian(density, hamiltonian) - damping[:, None, None, None] * density + coupled
    first_slope = derivative(rho)
    middle = rho + step_size * first_slope
    second_slope = derivative(middle)
    return rho + 0.5 * step_size * (first_slope + second_slope)
```

```python
import functools

import jax
import jax.numpy as jnp
from jax import lax
from jax.experimental import pallas as pl
from jax.experimental.pallas import tpu as pltpu
from jax.sharding import PartitionSpec as P

REACH = 4
STEP = 0.1
F32 = jnp.float32
BF16 = jnp.bfloat16
I32 = jnp.int32

SLOT = (1, 63)
TARGET = (7, 63)
MODE = (13, 31)
FLAG = (18, 1)
OCC = (19, 15)
CORE = (23, 1)
PLACE = (24, 3)

HEAVY = ((2, 0), (2, 1), (3, 0), (3, 1), (2, 2), (3, 2), (3, 3))
LIGHT = ((2, 2), (2, 3), (3, 3))
CROSSING = 4

VARIANTS = ((3, 2, 3), (4, 2, 3), (5, 3, 3), (7, 3, 4))


def split(value):
    high = value.astype(BF16)
    low = (value - high.astype(F32)).astype(BF16)
    return high, low


def flip(index, stride):
    return index + stride - 2 * stride * ((index // stride) % 2)


def put(field, value):
    return value << field[0]


def get(field, code):
    return (code >> field[0]) & field[1]


def distance_index(source, target, tier_size):
    d = lax.rem(source - target + tier_size, tier_size)
    return jnp.where(d <= REACH, d - 1, d - tier_size + 2 * REACH)


def plan_kernel(tier_size, mats, left_ref, count_ref, pair_ref, heavy_ref, light_ref, pick_ref):
    left_cap = left_ref.shape[1]
    places = 2 * REACH

    def clear(ref):
        def one(i, carry):
            ref[i] = jnp.int32(0)
            return carry

        lax.fori_loop(0, ref.shape[0], one, 0)

    clear(pair_ref)
    clear(heavy_ref)
    clear(light_ref)

    def block(b, carry):
        count = count_ref[b]
        for j in range(left_cap):
            source = left_ref[1, j, b]
            owner = lax.div(source, jnp.int32(mats))
            code = 1 + put(SLOT, source - owner * mats) + put(TARGET, left_ref[0, j, b])
            code = code + put(MODE, left_ref[2, j, b]) + put(FLAG, left_ref[3, j, b]) + put(OCC, left_ref[4, j, b])
            index = jnp.clip(distance_index(owner, b, tier_size), 0, places - 1)
            pair_ref[jnp.where(j < count, b * places + index, tier_size * places)] = code
        return carry

    lax.fori_loop(0, tier_size, block, 0)

    def chip(k, most):
        plane, half = k // 2, k % 2
        toward = 2 * half - 1

        def place(m):
            return jnp.where(half == 1, m, REACH - 1 - m)

        def fill(ref, width, pairs, step):
            other = lax.rem(plane + step + tier_size // REACH, tier_size // REACH)
            rank = jnp.int32(0)
            ranks = []
            for m_source, m_target in pairs:
                source = plane * REACH + place(m_source)
                target = other * REACH + place(m_target)
                code = pair_ref[target * places + distance_index(source, target, tier_size)]
                ref[k * width + rank] = code + put(CORE, source % 2) + put(PLACE, place(m_target))
                rank = rank + (code & 1)
                ranks.append(rank)
            ref[k * width + rank] = jnp.int32(0)
            return ranks

        heavy = fill(heavy_ref, 8, HEAVY, toward)
        light = fill(light_ref, 4, LIGHT, -toward)
        found = (heavy[-1], light[-1], heavy[CROSSING - 1])
        return tuple(jnp.maximum(x, y) for x, y in zip(most, found))

    most = lax.fori_loop(0, tier_size // 2, chip, (jnp.int32(0),) * 3)
    pick = jnp.int32(len(VARIANTS) - 1)
    for i in reversed(range(len(VARIANTS) - 1)):
        a, b, e = VARIANTS[i]
        pick = jnp.where((most[0] <= a) & (most[1] <= b) & (most[2] <= e), i, pick)
    pick_ref[0] = pick


def row_order(variant, colours):
    a, b, e = variant
    timed = [(1.0 + i, 0, "heavy", i) for i in range(a)]
    timed += [(1.2 + i, 1, "light", i) for i in range(b)]
    timed += [(3.1 + i, 2, "cross", i) for i in range(e)]
    lanes = [(kind, i) for _, _, kind, i in sorted(timed)]
    return [("plane", 0), ("plane", 1), ("colour", 1)] + lanes + [("colour", c) for c in range(2, colours)]


def kernel(
    tier_size,
    colours,
    variant,
    rho_any,
    ham_any,
    coup_any,
    bath_ref,
    damp_ref,
    match_ref,
    pair_ref,
    heavy_ref,
    light_ref,
    out_ref,
    rho_ref,
    ham_ref,
    coup_ref,
    load_sem,
    first_ref,
    term_ref,
    share_mine,
    share_other,
    packed,
    lanes,
    arrived,
    op_left,
    op_right,
    fact,
    share_send,
    share_recv,
    send_sem,
    recv_sem,
):
    loads = [
        pltpu.make_async_copy(rho_any, rho_ref, load_sem.at[0]),
        pltpu.make_async_copy(ham_any, ham_ref, load_sem.at[1]),
        pltpu.make_async_copy(coup_any, coup_ref, load_sem.at[2]),
    ]
    for load in loads:
        load.start()
    me = lax.axis_index("tier")
    mats = rho_ref.shape[0]
    order = rho_ref.shape[2]
    modes = coup_ref.shape[0]
    places = 2 * REACH
    a_lanes, b_lanes, e_lanes = variant
    rows = row_order(variant, colours)
    index_of = {row: i for i, row in enumerate(rows)}
    first_lane = 3
    last_lane = first_lane + a_lanes + b_lanes + e_lanes

    core = me % 2
    place = me % REACH
    half = place // 2
    toward = 2 * half - 1
    mate = flip(me, 1)
    across = flip(me, 2)
    beside = [across - core, across - core + 1]
    heavy_to = lax.rem(me + REACH * toward + tier_size, tier_size)
    light_to = lax.rem(me - REACH * toward + tier_size, tier_size)
    partners = [flip(me, 2**c) for c in range(colours)]

    greeted = [mate, beside[0], beside[1], heavy_to, light_to] + partners[2:]
    barrier = pltpu.get_barrier_semaphore()
    for device in greeted:
        pl.semaphore_signal(barrier, inc=1, device_id={"tier": device}, device_id_type=pl.DeviceIdType.MESH)
    pl.semaphore_wait(barrier, len(greeted))

    def remote(source, target, send, recv, device):
        return pltpu.make_async_remote_copy(
            src_ref=source,
            dst_ref=target,
            send_sem=send,
            recv_sem=recv,
            device_id={"tier": device},
            device_id_type=pl.DeviceIdType.MESH,
        )

    def pair_code(source, target):
        return pair_ref[target * places + distance_index(source, target, tier_size)]

    def match_code(c):
        return (
            1
            + put(TARGET, match_ref[c, 0])
            + put(SLOT, match_ref[c, 1])
            + put(MODE, match_ref[c, 2])
            + put(FLAG, match_ref[c, 3])
            + put(OCC, match_ref[c, 4])
        )

    def mine(code):
        return jnp.where(get(PLACE, code) == place, code, 0)

    heavy_from = light_to // 2
    light_from = heavy_to // 2
    cross_from = lax.rem(across + REACH * toward + tier_size, tier_size) // 2
    for i, (kind, number) in enumerate(rows):
        if kind == "plane":
            fact[i] = pair_code(beside[number], me)
        elif kind == "colour":
            fact[i] = match_code(number)
        elif kind == "heavy":
            fact[i] = mine(heavy_ref[heavy_from * 8 + number])
        elif kind == "light":
            fact[i] = mine(light_ref[light_from * 4 + number])
        else:
            fact[i] = mine(heavy_ref[cross_from * 8 + number])
    near = len(rows)
    fact[near] = match_code(0)
    fact[near + 1] = pair_code(mate, me)

    direct = [("colour", c) for c in range(colours - 1, 1, -1)] + [("colour", 1), ("plane", 0), ("plane", 1)]
    direct_to = partners[colours - 1 : 1 : -1] + [across] + beside
    far = len(direct) - 3

    def direct_slot(n):
        kind, number = direct[n]
        if kind == "colour":
            return match_ref[number, 0]
        return get(SLOT, pair_code(me, beside[number]))

    def direct_copy(n, stage, part):
        kind, number = direct[n]
        row = core if kind == "plane" else index_of[direct[n]]
        return remote(
            packed.at[n, part],
            arrived.at[stage, row, part],
            send_sem.at[stage, n, part],
            recv_sem.at[stage, row, part],
            direct_to[n],
        )

    outgoing = [("heavy", i) for i in range(a_lanes)] + [("light", i) for i in range(b_lanes)]
    outgoing = [row for row in rows if row in outgoing]

    def lane_copy(n, stage):
        row = index_of[outgoing[n]]
        return remote(
            lanes.at[n],
            arrived.at[stage, row, core],
            send_sem.at[stage, len(direct) + n, 0],
            recv_sem.at[stage, row, core],
            heavy_to if outgoing[n][0] == "heavy" else light_to,
        )

    def mate_copy(row, stage):
        return remote(
            arrived.at[stage, row, core],
            arrived.at[stage, row, core],
            send_sem.at[stage, len(direct) + row, 1],
            recv_sem.at[stage, row, core],
            mate,
        )

    def cross_copy(row, stage):
        landing = index_of[("cross", rows[row][1])]
        return remote(
            arrived.at[stage, row, core],
            arrived.at[stage, landing, core],
            send_sem.at[stage, len(direct) + row, 2],
            recv_sem.at[stage, landing, core],
            across,
        )

    def share_copies(source, stage):
        return [
            remote(source.at[:, 1 - core], share_mine.at[stage], share_send.at[stage, 0], share_recv.at[stage, 0], mate),
            remote(source.at[:, core], share_other.at[stage], share_send.at[stage, 1], share_recv.at[stage, 1], mate),
        ]

    def wait_part(row, part, stage):
        remote(
            arrived.at[stage, row, part],
            arrived.at[stage, row, part],
            send_sem.at[stage, 0, 0],
            recv_sem.at[stage, row, part],
            mate,
        ).wait_recv()

    def hand_on(row, stage):
        kind, number = rows[row]
        wait_part(row, core, stage)
        mate_copy(row, stage).start()
        if kind == "heavy" and number < e_lanes:
            cross_copy(row, stage).start()

    def products(value, left, right):
        re_high, re_low = split(value[0])
        im_high, im_low = split(value[1])
        column = jnp.concatenate(
            [
                jnp.concatenate([re_high, re_low, re_high], axis=0),
                jnp.concatenate([im_high, im_low, im_high], axis=0),
            ],
            axis=1,
        )
        row = jnp.concatenate(
            [
                jnp.concatenate([re_high, re_low, re_high], axis=1),
                jnp.concatenate([im_high, im_low, im_high], axis=1),
            ],
            axis=0,
        )
        p = jnp.dot(left, column, preferred_element_type=F32)
        r = jnp.dot(row, right, preferred_element_type=F32)
        return p[:, :order], p[:, order:], r[:order], r[order:]

    def add_row(code, value, scale, acc):
        weight, target, mode, occ = code & 1, get(TARGET, code), get(MODE, code), get(OCC, code)
        lower = get(FLAG, code) == 1
        a = jnp.where(lower, F32(1.0), bath_ref[0, mode])
        b = jnp.where(lower, F32(0.0), bath_ref[1, mode])
        p_re, p_im, r_re, r_im = products(value, op_left[mode], op_right[mode])
        root = jnp.sqrt(jnp.full((1, order), occ, I32).astype(F32)) * weight.astype(F32) * scale
        ca = root * a
        cb = root * b
        term_ref[0] = ca * (p_im - r_im) + cb * (p_re + r_re)
        term_ref[1] = cb * (p_im + r_im) - ca * (p_re - r_re)

        def add(s, carry):
            chosen = jnp.where(target == s, F32(1.0), F32(0.0))
            acc[s] = acc[s] + chosen * term_ref[...]
            return carry

        lax.fori_loop(0, mats, add, 0)

    def stage_rows(stage, source, scale, acc, own):
        shares = share_copies(source, stage)

        started = []
        for n in range(len(direct)):
            packed[n] = source[direct_slot(n)]
            if n == 1:
                direct_copy(0, stage, 0).start()
                shares[0].start()
            elif n > 1:
                for part in range(1 if n - 1 < far else 2):
                    direct_copy(n - 1, stage, part).start()
        for part in range(2):
            direct_copy(len(direct) - 1, stage, part).start()
        shares[1].start()

        own()

        shares[0].wait_recv()
        for n, row in enumerate(outgoing):
            if row[0] == "heavy":
                code = heavy_ref[(me // 2) * 8 + row[1]]
            else:
                code = light_ref[(me // 2) * 4 + row[1]]
            slot = get(SLOT, code)
            lanes[n] = jnp.where(get(CORE, code) == core, source[slot, core], share_mine[stage, slot])
            if n > 0:
                lane_copy(n - 1, stage).start()
        lane_copy(len(outgoing) - 1, stage).start()
        for n in range(far - 1, -1, -1):
            direct_copy(n, stage, 1).start()

        shares[1].wait_recv()

        def near_row(i, carry):
            code = fact[near + i]
            slot = get(SLOT, code)
            my_part = share_mine[stage, slot]
            other_part = share_other[stage, slot]
            is_real = core == 0
            value = (jnp.where(is_real, my_part, other_part), jnp.where(is_real, other_part, my_part))
            add_row(code, value, scale, acc)
            return carry

        lax.fori_loop(0, 2, near_row, 0)

        def row_step(i, carry):
            for row in range(first_lane, last_lane):
                @pl.when(i == row - 1)
                def _():
                    hand_on(row, stage)

            wait_part(i, 1 - core, stage)

            @pl.when((i < first_lane) | (i >= last_lane))
            def _():
                wait_part(i, core, stage)

            add_row(fact[i], arrived[stage, i], scale, acc)
            return carry

        lax.fori_loop(0, len(rows), row_step, 0)

        for share in shares:
            share.wait_send()
        for n in range(len(direct)):
            for part in range(2):
                direct_copy(n, stage, part).wait_send()
        for n in range(len(outgoing)):
            lane_copy(n, stage).wait_send()
        for row in range(first_lane, last_lane):
            mate_copy(row, stage).wait_send()
            kind, number = rows[row]
            if kind == "heavy" and number < e_lanes:
                cross_copy(row, stage).wait_send()

    def own_first():
        loads[1].wait()
        loads[2].wait()

        def prepare(k, carry):
            high, low = split(coup_ref[k])
            op_left[k] = jnp.concatenate([high, high, low], axis=1)
            op_right[k] = jnp.concatenate([high, high, low], axis=0)
            return carry

        lax.fori_loop(0, modes, prepare, 0)
        high, low = split(ham_ref[...])
        op_left[modes] = jnp.concatenate([high, high, low], axis=1)
        op_right[modes] = jnp.concatenate([high, high, low], axis=0)

        def own(n, carry):
            value = rho_ref[n]
            p_re, p_im, r_re, r_im = products(value, op_left[modes], op_right[modes])
            first_ref[n, 0] = (p_im - r_im) - damp_ref[n] * value[0]
            first_ref[n, 1] = (r_re - p_re) - damp_ref[n] * value[1]
            return carry

        lax.fori_loop(0, mats, own, 0)

    factor = F32(0.5 * STEP * STEP)

    def own_second():
        def own(n, carry):
            value = first_ref[n]
            p_re, p_im, r_re, r_im = products(value, op_left[modes], op_right[modes])
            out_ref[n, 0] = rho_ref[n, 0] + F32(STEP) * value[0] + factor * ((p_im - r_im) - damp_ref[n] * value[0])
            out_ref[n, 1] = rho_ref[n, 1] + F32(STEP) * value[1] + factor * ((r_re - p_re) - damp_ref[n] * value[1])
            return carry

        lax.fori_loop(0, mats, own, 0)

    loads[0].wait()
    stage_rows(0, rho_ref, F32(1.0), first_ref, own_first)
    stage_rows(1, first_ref, factor, out_ref, own_second)


def body(tier_size, rho, hamiltonian, couplings, bath_coef, damping, match_edges, left_rows, left_count):
    mats, _, order, _ = rho.shape
    modes = couplings.shape[0]
    table = match_edges.reshape(-1, match_edges.shape[-1])
    colours = table.shape[0]
    vmem = pl.BlockSpec(memory_space=pltpu.VMEM)
    hbm = pl.BlockSpec(memory_space=pl.ANY)
    smem = pl.BlockSpec(memory_space=pltpu.SMEM)

    pair, heavy, light, pick = pl.pallas_call(
        functools.partial(plan_kernel, tier_size, mats),
        out_shape=[
            jax.ShapeDtypeStruct((tier_size * 2 * REACH + 1,), I32),
            jax.ShapeDtypeStruct((tier_size // 2 * 8,), I32),
            jax.ShapeDtypeStruct((tier_size // 2 * 4,), I32),
            jax.ShapeDtypeStruct((1,), I32),
        ],
        in_specs=[smem, smem],
        out_specs=[smem] * 4,
    )(left_rows.transpose(2, 1, 0), left_count)

    def step(number, variant):
        a, b, e = variant
        rows = len(row_order(variant, colours))
        direct = colours + 1
        return pl.pallas_call(
            functools.partial(kernel, tier_size, colours, variant),
            out_shape=pltpu.VMEM(rho.shape, F32),
            in_specs=[hbm, hbm, hbm] + [smem] * 6,
            out_specs=vmem,
            scratch_shapes=[
                pltpu.VMEM(rho.shape, F32),
                pltpu.VMEM(hamiltonian.shape, F32),
                pltpu.VMEM(couplings.shape, F32),
                pltpu.SemaphoreType.DMA((3,)),
                pltpu.VMEM(rho.shape, F32),
                pltpu.VMEM((2, order, order), F32),
                pltpu.VMEM((2, mats, order, order), F32),
                pltpu.VMEM((2, mats, order, order), F32),
                pltpu.VMEM((direct, 2, order, order), F32),
                pltpu.VMEM((a + b, order, order), F32),
                pltpu.VMEM((2, rows, 2, order, order), F32),
                pltpu.VMEM((modes + 1, order, 3 * order), BF16),
                pltpu.VMEM((modes + 1, 3 * order, order), BF16),
                pltpu.SMEM((rows + 2,), I32),
                pltpu.SemaphoreType.DMA((2, 2)),
                pltpu.SemaphoreType.DMA((2, 2)),
                pltpu.SemaphoreType.DMA((2, direct + rows, 3)),
                pltpu.SemaphoreType.DMA((2, rows, 2)),
            ],
            compiler_params=pltpu.CompilerParams(
                collective_id=number, has_side_effects=True, vmem_limit_bytes=58 * 1024 * 1024
            ),
        )

    return lax.switch(
        pick[0],
        [step(i, variant) for i, variant in enumerate(VARIANTS)],
        rho,
        hamiltonian,
        couplings,
        bath_coef.T,
        damping,
        table,
        pair,
        heavy,
        light,
    )


def solution(mesh):
    placed = (
        P(("groups", "tier"), None, None, None),
        P(),
        P(),
        P("groups", None),
        P(("groups", "tier")),
        P("tier", None, None, None),
        P(),
        P(),
    )
    return jax.shard_map(
        functools.partial(body, mesh.shape["tier"]),
        mesh=mesh,
        in_specs=placed,
        out_specs=P(("groups", "tier"), None, None, None),
        check_vma=False,
    )
```

```python
import functools

import jax
import jax.numpy as jnp
from jax import lax
from jax.experimental import pallas as pl
from jax.experimental.pallas import tpu as pltpu
from jax.sharding import PartitionSpec as P

REACH = 4
STEP = 0.1
F32 = jnp.float32
BF16 = jnp.bfloat16
I32 = jnp.int32

SLOT = (1, 63)
TARGET = (7, 63)
MODE = (13, 31)
FLAG = (18, 1)
OCC = (19, 15)
CORE = (23, 1)
PLACE = (24, 3)

HEAVY = ((2, 0), (2, 1), (3, 0), (3, 1), (2, 2), (3, 2), (3, 3))
LIGHT = ((2, 2), (2, 3), (3, 3))
CROSSING = 4
LEVEL = ((2, 0), (2, 1), (3, 0), (3, 1))
WIDTH = 8

VARIANTS = (
    (3, 2, 2, 1, 2, 3),
    (4, 2, 3, 1, 3, 3),
    (3, 2, 3, 2, 3, 3),
    (4, 2, 4, 2, 3, 4),
    (5, 3, 3, 1, 4, 3),
    (3, 3, 3, 3, 3, 4),
    (5, 3, 4, 2, 4, 4),
    (4, 2, 5, 3, 4, 3),
    (7, 3, 7, 3, 4, 4),
)


def split(value):
    high = value.astype(BF16)
    low = (value - high.astype(F32)).astype(BF16)
    return high, low


def flip(index, stride):
    return index + stride - 2 * stride * ((index // stride) % 2)


def put(field, value):
    return value << field[0]


def get(field, code):
    return (code >> field[0]) & field[1]


def distance_index(source, target, tier_size):
    d = lax.rem(source - target + tier_size, tier_size)
    return jnp.where(d <= REACH, d - 1, d - tier_size + 2 * REACH)


def plan_kernel(tier_size, mats, left_ref, count_ref, pair_ref, heavy_ref, light_ref, level_ref, pick_ref):
    left_cap = left_ref.shape[1]
    places = 2 * REACH
    planes = tier_size // REACH

    for ref in (pair_ref, heavy_ref, light_ref, level_ref):
        for i in range(ref.shape[0]):
            ref[i] = jnp.int32(0)

    for b in range(tier_size):
        count = count_ref[b]
        for j in range(left_cap):
            source = left_ref[1, j, b]
            owner = lax.div(source, jnp.int32(mats))
            code = 1 + put(SLOT, source - owner * mats) + put(TARGET, left_ref[0, j, b])
            code = code + put(MODE, left_ref[2, j, b]) + put(FLAG, left_ref[3, j, b]) + put(OCC, left_ref[4, j, b])
            index = jnp.clip(distance_index(owner, b, tier_size), 0, places - 1)
            pair_ref[jnp.where(j < count, b * places + index, tier_size * places)] = code

    most = [jnp.int32(0)] * 6
    for k in range(tier_size // 2):
        plane, half = k // 2, k % 2
        toward = 2 * half - 1

        def place(m):
            return m if half == 1 else REACH - 1 - m

        def fill(ref, pairs, other):
            rank = jnp.int32(k * WIDTH)
            ranks = []
            for m_source, m_target in pairs:
                source = plane * REACH + place(m_source)
                target = other % planes * REACH + place(m_target)
                d = (source - target) % tier_size
                index = d - 1 if d <= REACH else d - tier_size + places
                code = pair_ref[target * places + index]
                ref[rank] = code + ((source % 2) << CORE[0]) + (place(m_target) << PLACE[0])
                rank = rank + (code & 1)
                ranks.append(rank - k * WIDTH)
            ref[rank] = jnp.int32(0)
            return ranks

        heavy = fill(heavy_ref, HEAVY, plane + toward)
        light = fill(light_ref, LIGHT, plane - toward)
        level = fill(level_ref, LEVEL, plane)
        for at, step, found in ((0, toward, heavy), (1, -toward, light)):
            if not 0 <= plane + step < planes:
                at += 2
            most[at] = jnp.maximum(most[at], found[-1])
        most[4] = jnp.maximum(most[4], heavy[CROSSING - 1])
        most[5] = jnp.maximum(most[5], level[-1])

    pick = jnp.int32(len(VARIANTS) - 1)
    for i in reversed(range(len(VARIANTS) - 1)):
        fits = most[0] <= VARIANTS[i][0]
        for at in range(1, 6):
            fits = fits & (most[at] <= VARIANTS[i][at])
        pick = jnp.where(fits, i, pick)
    pick_ref[0] = pick


def row_order(variant, colours):
    a, b, a_wrap, b_wrap, e, f = variant
    timed = [(0.6 + i, 0, "level", i) for i in range(f)]
    timed += [(1.0 + i, 1, "heavy", i) for i in range(max(a, a_wrap))]
    timed += [(1.2 + i, 2, "light", i) for i in range(max(b, b_wrap))]
    timed += [(3.1 + i, 3, "cross", i) for i in range(e)]
    lanes = [(kind, i) for _, _, kind, i in sorted(timed)]
    return [("colour", 1)] + lanes + [("colour", c) for c in range(2, colours)]


def kernel(
    tier_size,
    colours,
    variant,
    rho_any,
    ham_any,
    coup_any,
    bath_ref,
    damp_ref,
    match_ref,
    pair_ref,
    heavy_ref,
    light_ref,
    level_ref,
    out_ref,
    state,
    ham_ref,
    coup_ref,
    load_sem,
    term_ref,
    share_mine,
    share_other,
    packed,
    lanes,
    arrived,
    op_left,
    op_right,
    fact,
    share_send,
    share_recv,
    send_sem,
    recv_sem,
):
    loads = [
        pltpu.make_async_copy(rho_any, state.at[0], load_sem.at[0]),
        pltpu.make_async_copy(ham_any, ham_ref, load_sem.at[1]),
        pltpu.make_async_copy(coup_any, coup_ref, load_sem.at[2]),
    ]
    for load in loads:
        load.start()
    me = lax.axis_index("tier")
    mats = rho_any.shape[0]
    order = rho_any.shape[2]
    modes = coup_ref.shape[0]
    places = 2 * REACH
    a_lanes, b_lanes, a_wrap, b_wrap, e_lanes, _ = variant
    rows = row_order(variant, colours)
    index_of = {row: i for i, row in enumerate(rows)}
    lane_rows = [i for i, (kind, _) in enumerate(rows) if kind != "colour"]

    core = me % 2
    place = me % REACH
    half = place // 2
    toward = 2 * half - 1
    mate = flip(me, 1)
    across = flip(me, 2)
    plane = me // REACH
    planes = tier_size // REACH
    heavy_to = lax.rem(me + REACH * toward + tier_size, tier_size)
    light_to = lax.rem(me - REACH * toward + tier_size, tier_size)
    partners = [flip(me, 2**c) for c in range(colours)]

    heavy_wraps = (plane + toward < 0) | (plane + toward >= planes)
    light_wraps = (plane - toward < 0) | (plane - toward >= planes)

    greeted = [mate, across, heavy_to, light_to] + partners[2:]
    barrier = pltpu.get_barrier_semaphore()
    for device in greeted:
        pl.semaphore_signal(barrier, inc=1, device_id={"tier": device}, device_id_type=pl.DeviceIdType.MESH)
    pl.semaphore_wait(barrier, len(greeted))

    def remote(source, target, send, recv, device):
        return pltpu.make_async_remote_copy(
            src_ref=source,
            dst_ref=target,
            send_sem=send,
            recv_sem=recv,
            device_id={"tier": device},
            device_id_type=pl.DeviceIdType.MESH,
        )

    def lane_used(kind, number, wraps):
        line, wrap = {"heavy": (a_lanes, a_wrap), "light": (b_lanes, b_wrap)}[kind]
        if number < min(line, wrap):
            return None
        return jnp.logical_not(wraps) if number < line else wraps

    def when(condition):
        if condition is None:
            return lambda run: run()
        return pl.when(condition)

    def lands(row):
        kind, number = rows[row]
        if kind == "heavy":
            return lane_used("heavy", number, light_wraps)
        if kind == "light":
            return lane_used("light", number, heavy_wraps)
        if kind == "cross":
            return lane_used("heavy", number, heavy_wraps)
        return None

    def pair_code(source, target):
        return pair_ref[target * places + distance_index(source, target, tier_size)]

    def match_code(c):
        return (
            1
            + put(TARGET, match_ref[c, 0])
            + put(SLOT, match_ref[c, 1])
            + put(MODE, match_ref[c, 2])
            + put(FLAG, match_ref[c, 3])
            + put(OCC, match_ref[c, 4])
        )

    def mine(code):
        return jnp.where(get(PLACE, code) == place, code, 0)

    heavy_from = light_to // 2
    light_from = heavy_to // 2
    cross_from = lax.rem(across + REACH * toward + tier_size, tier_size) // 2
    for i, (kind, number) in enumerate(rows):
        if kind == "colour":
            fact[i] = match_code(number)
        elif kind == "level":
            fact[i] = mine(level_ref[(across // 2) * WIDTH + number])
        elif kind == "heavy":
            fact[i] = mine(heavy_ref[heavy_from * WIDTH + number])
        elif kind == "light":
            fact[i] = mine(light_ref[light_from * WIDTH + number])
        else:
            fact[i] = mine(heavy_ref[cross_from * WIDTH + number])
    near = len(rows)
    fact[near] = match_code(0)
    fact[near + 1] = pair_code(mate, me)

    direct = list(range(colours - 1, 0, -1))

    def direct_copy(n, stage, part):
        row = index_of[("colour", direct[n])]
        return remote(
            packed.at[n, part],
            arrived.at[stage, row, part],
            send_sem.at[stage, n, part],
            recv_sem.at[stage, row, part],
            partners[direct[n]],
        )

    outgoing = [row for row in rows if row[0] in ("level", "heavy", "light")]

    def leaves(n):
        kind, number = outgoing[n]
        if kind == "level":
            return None
        return lane_used(kind, number, heavy_wraps if kind == "heavy" else light_wraps)

    def lane_copy(n, stage):
        row = index_of[outgoing[n]]
        return remote(
            lanes.at[n],
            arrived.at[stage, row, core],
            send_sem.at[stage, len(direct) + n, 0],
            recv_sem.at[stage, row, core],
            {"level": across, "heavy": heavy_to, "light": light_to}[outgoing[n][0]],
        )

    def mate_copy(row, stage):
        return remote(
            arrived.at[stage, row, core],
            arrived.at[stage, row, core],
            send_sem.at[stage, len(direct) + row, 1],
            recv_sem.at[stage, row, core],
            mate,
        )

    def cross_copy(row, stage):
        landing = index_of[("cross", rows[row][1])]
        return remote(
            arrived.at[stage, row, core],
            arrived.at[stage, landing, core],
            send_sem.at[stage, len(direct) + row, 2],
            recv_sem.at[stage, landing, core],
            across,
        )

    def share_copies(source, stage):
        return [
            remote(source.at[:, 1 - core], share_mine.at[stage], share_send.at[stage, 0], share_recv.at[stage, 0], mate),
            remote(source.at[:, core], share_other.at[stage], share_send.at[stage, 1], share_recv.at[stage, 1], mate),
        ]

    def wait_part(row, part, stage):
        remote(
            arrived.at[stage, row, part],
            arrived.at[stage, row, part],
            send_sem.at[stage, 0, 0],
            recv_sem.at[stage, row, part],
            mate,
        ).wait_recv()

    def hand_on(row, stage):
        kind, number = rows[row]
        wait_part(row, core, stage)
        mate_copy(row, stage).start()
        if kind == "heavy" and number < e_lanes:
            cross_copy(row, stage).start()

    def products(value, left, right):
        re_high, re_low = split(value[0])
        im_high, im_low = split(value[1])
        column = jnp.concatenate(
            [
                jnp.concatenate([re_high, re_low, re_high], axis=0),
                jnp.concatenate([im_high, im_low, im_high], axis=0),
            ],
            axis=1,
        )
        row = jnp.concatenate(
            [
                jnp.concatenate([re_high, re_low, re_high], axis=1),
                jnp.concatenate([im_high, im_low, im_high], axis=1),
            ],
            axis=0,
        )
        p = jnp.dot(left, column, preferred_element_type=F32)
        r = jnp.dot(row, right, preferred_element_type=F32)
        return p[:, :order], p[:, order:], r[:order], r[order:]

    def add_row(code, value, scale, stage):
        weight, target, mode, occ = code & 1, get(TARGET, code), get(MODE, code), get(OCC, code)
        lower = get(FLAG, code) == 1
        a = jnp.where(lower, F32(1.0), bath_ref[0, mode])
        b = jnp.where(lower, F32(0.0), bath_ref[1, mode])
        p_re, p_im, r_re, r_im = products(value, op_left[mode], op_right[mode])
        root = jnp.sqrt(jnp.full((1, order), occ, I32).astype(F32)) * weight.astype(F32) * scale
        ca = root * a
        cb = root * b
        term_ref[0] = ca * (p_im - r_im) + cb * (p_re + r_re)
        term_ref[1] = cb * (p_im + r_im) - ca * (p_re - r_re)

        def add_to(acc):
            def add(s, carry):
                chosen = jnp.where(target == s, F32(1.0), F32(0.0))
                acc[s] = acc[s] + chosen * term_ref[...]
                return carry

            lax.fori_loop(0, mats, add, 0)

        pl.when(stage == 0)(functools.partial(add_to, state.at[1]))
        pl.when(stage == 1)(functools.partial(add_to, out_ref))

    def prepare_operators():
        loads[1].wait()
        loads[2].wait()

        def prepare(k, carry):
            high, low = split(coup_ref[k])
            op_left[k] = jnp.concatenate([high, high, low], axis=1)
            op_right[k] = jnp.concatenate([high, high, low], axis=0)
            return carry

        lax.fori_loop(0, modes, prepare, 0)
        high, low = split(ham_ref[...])
        op_left[modes] = jnp.concatenate([high, high, low], axis=1)
        op_right[modes] = jnp.concatenate([high, high, low], axis=0)

    half_square = F32(0.5 * STEP * STEP)

    def stage_rows(stage, carry):
        source = state.at[stage]
        scale = jnp.where(stage == 0, F32(1.0), half_square)
        shares = share_copies(source, stage)

        for n in range(len(direct)):
            packed[n] = source[match_ref[direct[n], 0]]
            if n > 0:
                direct_copy(n - 1, stage, 0).start()
            if n == 1:
                shares[0].start()
        for part in range(2):
            direct_copy(len(direct) - 1, stage, part).start()
        shares[1].start()

        @pl.when(stage == 0)
        def _():
            prepare_operators()

        def own(n, carry):
            value = source[n]
            p_re, p_im, r_re, r_im = products(value, op_left[modes], op_right[modes])
            slope_re = (p_im - r_im) - damp_ref[n] * value[0]
            slope_im = (r_re - p_re) - damp_ref[n] * value[1]

            @pl.when(stage == 0)
            def _():
                state[1, n, 0] = slope_re
                state[1, n, 1] = slope_im

            @pl.when(stage == 1)
            def _():
                out_ref[n, 0] = state[0, n, 0] + F32(STEP) * value[0] + half_square * slope_re
                out_ref[n, 1] = state[0, n, 1] + F32(STEP) * value[1] + half_square * slope_im

            return carry

        lax.fori_loop(0, mats, own, 0)

        shares[0].wait_recv()
        tables = {"level": level_ref, "heavy": heavy_ref, "light": light_ref}
        for n, (kind, number) in enumerate(outgoing):
            code = tables[kind][(me // 2) * WIDTH + number]
            slot = get(SLOT, code)
            lanes[n] = jnp.where(get(CORE, code) == core, source[slot, core], share_mine[stage, slot])
            if n > 0:
                when(leaves(n - 1))(lane_copy(n - 1, stage).start)
        when(leaves(len(outgoing) - 1))(lane_copy(len(outgoing) - 1, stage).start)
        for n in range(len(direct) - 2, -1, -1):
            direct_copy(n, stage, 1).start()

        shares[1].wait_recv()

        def near_row(i, carry):
            code = fact[near + i]
            slot = get(SLOT, code)
            my_part = share_mine[stage, slot]
            other_part = share_other[stage, slot]
            is_real = core == 0
            value = (jnp.where(is_real, my_part, other_part), jnp.where(is_real, other_part, my_part))
            add_row(code, value, scale, stage)
            return carry

        lax.fori_loop(0, 2, near_row, 0)

        def row_step(i, carry):
            there = i >= 0
            is_lane = i < 0
            for row in lane_rows:
                used = lands(row)
                now = i == row - 1
                when(now if used is None else now & used)(functools.partial(hand_on, row, stage))
                is_lane = is_lane | (i == row)
                if used is not None:
                    there = there & ((i != row) | used)

            @pl.when(there)
            def _():
                wait_part(i, 1 - core, stage)

                @pl.when(jnp.logical_not(is_lane))
                def _():
                    wait_part(i, core, stage)

                add_row(fact[i], arrived[stage, i], scale, stage)

            return carry

        lax.fori_loop(0, len(rows), row_step, 0)

        for share in shares:
            share.wait_send()
        for n in range(len(direct)):
            for part in range(2):
                direct_copy(n, stage, part).wait_send()
        for n in range(len(outgoing)):
            when(leaves(n))(lane_copy(n, stage).wait_send)
        for row in lane_rows:
            kind, number = rows[row]

            def sent():
                mate_copy(row, stage).wait_send()
                if kind == "heavy" and number < e_lanes:
                    cross_copy(row, stage).wait_send()

            when(lands(row))(sent)
        return carry

    loads[0].wait()
    lax.fori_loop(0, 2, stage_rows, 0)


def body(tier_size, rho, hamiltonian, couplings, bath_coef, damping, match_edges, left_rows, left_count):
    mats, _, order, _ = rho.shape
    modes = couplings.shape[0]
    table = match_edges.reshape(-1, match_edges.shape[-1])
    colours = table.shape[0]
    vmem = pl.BlockSpec(memory_space=pltpu.VMEM)
    hbm = pl.BlockSpec(memory_space=pl.ANY)
    smem = pl.BlockSpec(memory_space=pltpu.SMEM)

    pair, heavy, light, level, pick = pl.pallas_call(
        functools.partial(plan_kernel, tier_size, mats),
        out_shape=[
            jax.ShapeDtypeStruct((tier_size * 2 * REACH + 1,), I32),
            jax.ShapeDtypeStruct((tier_size // 2 * WIDTH,), I32),
            jax.ShapeDtypeStruct((tier_size // 2 * WIDTH,), I32),
            jax.ShapeDtypeStruct((tier_size // 2 * WIDTH,), I32),
            jax.ShapeDtypeStruct((1,), I32),
        ],
        in_specs=[smem, smem],
        out_specs=[smem] * 5,
    )(left_rows.transpose(2, 1, 0), left_count)

    def step(number, variant):
        order_of_rows = row_order(variant, colours)
        rows = len(order_of_rows)
        lanes = sum(kind in ("level", "heavy", "light") for kind, _ in order_of_rows)
        direct = colours - 1
        return pl.pallas_call(
            functools.partial(kernel, tier_size, colours, variant),
            out_shape=pltpu.VMEM(rho.shape, F32),
            in_specs=[hbm, hbm, hbm] + [smem] * 7,
            out_specs=vmem,
            scratch_shapes=[
                pltpu.VMEM((2,) + rho.shape, F32),
                pltpu.VMEM(hamiltonian.shape, F32),
                pltpu.VMEM(couplings.shape, F32),
                pltpu.SemaphoreType.DMA((3,)),
                pltpu.VMEM((2, order, order), F32),
                pltpu.VMEM((2, mats, order, order), F32),
                pltpu.VMEM((2, mats, order, order), F32),
                pltpu.VMEM((direct, 2, order, order), F32),
                pltpu.VMEM((lanes, order, order), F32),
                pltpu.VMEM((2, rows, 2, order, order), F32),
                pltpu.VMEM((modes + 1, order, 3 * order), BF16),
                pltpu.VMEM((modes + 1, 3 * order, order), BF16),
                pltpu.SMEM((rows + 2,), I32),
                pltpu.SemaphoreType.DMA((2, 2)),
                pltpu.SemaphoreType.DMA((2, 2)),
                pltpu.SemaphoreType.DMA((2, direct + rows, 3)),
                pltpu.SemaphoreType.DMA((2, rows, 2)),
            ],
            compiler_params=pltpu.CompilerParams(
                collective_id=number, has_side_effects=True, vmem_limit_bytes=58 * 1024 * 1024
            ),
        )

    return lax.switch(
        pick[0],
        [step(i, variant) for i, variant in enumerate(VARIANTS)],
        rho,
        hamiltonian,
        couplings,
        bath_coef.T,
        damping,
        table,
        pair,
        heavy,
        light,
        level,
    )


def solution(mesh):
    placed = (
        P(("groups", "tier"), None, None, None),
        P(),
        P(),
        P("groups", None),
        P(("groups", "tier")),
        P("tier", None, None, None),
        P(),
        P(),
    )
    return jax.shard_map(
        functools.partial(body, mesh.shape["tier"]),
        mesh=mesh,
        in_specs=placed,
        out_specs=P(("groups", "tier"), None, None, None),
        check_vma=False,
    )
```

```python
import functools

import jax
import jax.numpy as jnp
from jax import lax
from jax.experimental import pallas as pl
from jax.experimental.pallas import tpu as pltpu
from jax.sharding import PartitionSpec as P

REACH = 4
STEP = 0.1
F32 = jnp.float32
BF16 = jnp.bfloat16
I32 = jnp.int32

SLOT = (1, 63)
TARGET = (7, 63)
MODE = (13, 31)
FLAG = (18, 1)
OCC = (19, 15)
CORE = (23, 1)
PLACE = (24, 3)

HEAVY = ((2, 0), (2, 1), (3, 0), (3, 1), (2, 2), (3, 2), (3, 3))
LIGHT = ((2, 2), (2, 3), (3, 3))
CROSSING = 4
LEVEL = ((2, 0), (2, 1), (3, 0), (3, 1))
WIDTH = 8

VARIANTS = (
    (3, 2, 2, 1, 2, 3),
    (4, 2, 3, 1, 3, 3),
    (3, 2, 3, 2, 3, 3),
    (4, 2, 4, 2, 3, 4),
    (5, 3, 3, 1, 4, 3),
    (3, 3, 3, 3, 3, 4),
    (5, 3, 4, 2, 4, 4),
    (4, 2, 5, 3, 4, 3),
    (7, 3, 7, 3, 4, 4),
)


def split(value):
    high = value.astype(BF16)
    low = (value - high.astype(F32)).astype(BF16)
    return high, low


def flip(index, stride):
    return index + stride - 2 * stride * ((index // stride) % 2)


def put(field, value):
    return value << field[0]


def get(field, code):
    return (code >> field[0]) & field[1]


def distance_index(source, target, tier_size):
    d = lax.rem(source - target + tier_size, tier_size)
    return jnp.where(d <= REACH, d - 1, d - tier_size + 2 * REACH)


def plan_kernel(tier_size, mats, left_ref, count_ref, pair_ref, heavy_ref, light_ref, level_ref, pick_ref):
    left_cap = left_ref.shape[1]
    places = 2 * REACH
    planes = tier_size // REACH

    for ref in (pair_ref, heavy_ref, light_ref, level_ref):
        for i in range(ref.shape[0]):
            ref[i] = jnp.int32(0)

    for b in range(tier_size):
        count = count_ref[b]
        for j in range(left_cap):
            source = left_ref[1, j, b]
            owner = lax.div(source, jnp.int32(mats))
            code = 1 + put(SLOT, source - owner * mats) + put(TARGET, left_ref[0, j, b])
            code = code + put(MODE, left_ref[2, j, b]) + put(FLAG, left_ref[3, j, b]) + put(OCC, left_ref[4, j, b])
            index = jnp.clip(distance_index(owner, b, tier_size), 0, places - 1)
            pair_ref[jnp.where(j < count, b * places + index, tier_size * places)] = code

    most = [jnp.int32(0)] * 6
    for k in range(tier_size // 2):
        plane, half = k // 2, k % 2
        toward = 2 * half - 1

        def place(m):
            return m if half == 1 else REACH - 1 - m

        def fill(ref, pairs, other):
            rank = jnp.int32(k * WIDTH)
            ranks = []
            for m_source, m_target in pairs:
                source = plane * REACH + place(m_source)
                target = other % planes * REACH + place(m_target)
                d = (source - target) % tier_size
                index = d - 1 if d <= REACH else d - tier_size + places
                code = pair_ref[target * places + index]
                ref[rank] = code + ((source % 2) << CORE[0]) + (place(m_target) << PLACE[0])
                rank = rank + (code & 1)
                ranks.append(rank - k * WIDTH)
            ref[rank] = jnp.int32(0)
            return ranks

        heavy = fill(heavy_ref, HEAVY, plane + toward)
        light = fill(light_ref, LIGHT, plane - toward)
        level = fill(level_ref, LEVEL, plane)
        for at, step, found in ((0, toward, heavy), (1, -toward, light)):
            if not 0 <= plane + step < planes:
                at += 2
            most[at] = jnp.maximum(most[at], found[-1])
        most[4] = jnp.maximum(most[4], heavy[CROSSING - 1])
        most[5] = jnp.maximum(most[5], level[-1])

    pick = jnp.int32(len(VARIANTS) - 1)
    for i in reversed(range(len(VARIANTS) - 1)):
        fits = most[0] <= VARIANTS[i][0]
        for at in range(1, 6):
            fits = fits & (most[at] <= VARIANTS[i][at])
        pick = jnp.where(fits, i, pick)
    pick_ref[0] = pick


def row_order(variant, colours):
    a, b, a_wrap, b_wrap, e, f = variant
    timed = [(0.6 + i, 0, "level", i) for i in range(f)]
    timed += [(1.0 + i, 1, "heavy", i) for i in range(max(a, a_wrap))]
    timed += [(1.2 + i, 2, "light", i) for i in range(max(b, b_wrap))]
    timed += [(3.1 + i, 3, "cross", i) for i in range(e)]
    lanes = [(kind, i) for _, _, kind, i in sorted(timed)]
    return [("colour", 1)] + lanes + [("colour", c) for c in range(colours - 1, 1, -1)]


def kernel(
    tier_size,
    colours,
    variant,
    rho_any,
    ham_any,
    coup_any,
    bath_ref,
    damp_ref,
    match_ref,
    pair_ref,
    heavy_ref,
    light_ref,
    level_ref,
    out_ref,
    state,
    ham_ref,
    coup_ref,
    load_sem,
    term_ref,
    share_mine,
    share_other,
    packed,
    lanes,
    arrived,
    op_left,
    op_right,
    fact,
    share_send,
    share_recv,
    send_sem,
    recv_sem,
):
    loads = [
        pltpu.make_async_copy(rho_any, state.at[0], load_sem.at[0]),
        pltpu.make_async_copy(ham_any, ham_ref, load_sem.at[1]),
        pltpu.make_async_copy(coup_any, coup_ref, load_sem.at[2]),
    ]
    for load in loads:
        load.start()
    me = lax.axis_index("tier")
    mats = rho_any.shape[0]
    order = rho_any.shape[2]
    modes = coup_ref.shape[0]
    places = 2 * REACH
    a_lanes, b_lanes, a_wrap, b_wrap, e_lanes, _ = variant
    rows = row_order(variant, colours)
    index_of = {row: i for i, row in enumerate(rows)}
    lane_rows = [i for i, (kind, _) in enumerate(rows) if kind != "colour"]

    core = me % 2
    place = me % REACH
    half = place // 2
    toward = 2 * half - 1
    mate = flip(me, 1)
    across = flip(me, 2)
    plane = me // REACH
    planes = tier_size // REACH
    heavy_to = lax.rem(me + REACH * toward + tier_size, tier_size)
    light_to = lax.rem(me - REACH * toward + tier_size, tier_size)
    partners = [flip(me, 2**c) for c in range(colours)]

    heavy_wraps = (plane + toward < 0) | (plane + toward >= planes)
    light_wraps = (plane - toward < 0) | (plane - toward >= planes)

    greeted = [mate, across, heavy_to, light_to] + partners[2:]
    barrier = pltpu.get_barrier_semaphore()
    for device in greeted:
        pl.semaphore_signal(barrier, inc=1, device_id={"tier": device}, device_id_type=pl.DeviceIdType.MESH)
    pl.semaphore_wait(barrier, len(greeted))

    def remote(source, target, send, recv, device):
        return pltpu.make_async_remote_copy(
            src_ref=source,
            dst_ref=target,
            send_sem=send,
            recv_sem=recv,
            device_id={"tier": device},
            device_id_type=pl.DeviceIdType.MESH,
        )

    def lane_used(kind, number, wraps):
        line, wrap = {"heavy": (a_lanes, a_wrap), "light": (b_lanes, b_wrap)}[kind]
        if number < min(line, wrap):
            return None
        return jnp.logical_not(wraps) if number < line else wraps

    def when(condition):
        if condition is None:
            return lambda run: run()
        return pl.when(condition)

    def lands(row):
        kind, number = rows[row]
        if kind == "heavy":
            return lane_used("heavy", number, light_wraps)
        if kind == "light":
            return lane_used("light", number, heavy_wraps)
        if kind == "cross":
            return lane_used("heavy", number, heavy_wraps)
        return None

    def pair_code(source, target):
        return pair_ref[target * places + distance_index(source, target, tier_size)]

    def match_code(c):
        return (
            1
            + put(TARGET, match_ref[c, 0])
            + put(SLOT, match_ref[c, 1])
            + put(MODE, match_ref[c, 2])
            + put(FLAG, match_ref[c, 3])
            + put(OCC, match_ref[c, 4])
        )

    def mine(code):
        return jnp.where(get(PLACE, code) == place, code, 0)

    heavy_from = light_to // 2
    light_from = heavy_to // 2
    cross_from = lax.rem(across + REACH * toward + tier_size, tier_size) // 2
    for i, (kind, number) in enumerate(rows):
        if kind == "colour":
            fact[i] = match_code(number)
        elif kind == "level":
            fact[i] = mine(level_ref[(across // 2) * WIDTH + number])
        elif kind == "heavy":
            fact[i] = mine(heavy_ref[heavy_from * WIDTH + number])
        elif kind == "light":
            fact[i] = mine(light_ref[light_from * WIDTH + number])
        else:
            fact[i] = mine(heavy_ref[cross_from * WIDTH + number])
    near = len(rows)
    fact[near] = match_code(0)
    fact[near + 1] = pair_code(mate, me)

    direct = list(range(colours - 1, 0, -1))

    def direct_copy(n, stage, part):
        row = index_of[("colour", direct[n])]
        return remote(
            packed.at[n, part],
            arrived.at[stage, row, part],
            send_sem.at[stage, n, part],
            recv_sem.at[stage, row, part],
            partners[direct[n]],
        )

    outgoing = [row for row in rows if row[0] in ("level", "heavy", "light")]

    def leaves(n):
        kind, number = outgoing[n]
        if kind == "level":
            return None
        return lane_used(kind, number, heavy_wraps if kind == "heavy" else light_wraps)

    def lane_copy(n, stage):
        row = index_of[outgoing[n]]
        return remote(
            lanes.at[n],
            arrived.at[stage, row, core],
            send_sem.at[stage, len(direct) + n, 0],
            recv_sem.at[stage, row, core],
            {"level": across, "heavy": heavy_to, "light": light_to}[outgoing[n][0]],
        )

    def mate_copy(row, stage):
        return remote(
            arrived.at[stage, row, core],
            arrived.at[stage, row, core],
            send_sem.at[stage, len(direct) + row, 1],
            recv_sem.at[stage, row, core],
            mate,
        )

    def cross_copy(row, stage):
        landing = index_of[("cross", rows[row][1])]
        return remote(
            arrived.at[stage, row, core],
            arrived.at[stage, landing, core],
            send_sem.at[stage, len(direct) + row, 2],
            recv_sem.at[stage, landing, core],
            across,
        )

    def share_copies(source, stage):
        return [
            remote(source.at[:, 1 - core], share_mine.at[stage], share_send.at[stage, 0], share_recv.at[stage, 0], mate),
            remote(source.at[:, core], share_other.at[stage], share_send.at[stage, 1], share_recv.at[stage, 1], mate),
        ]

    def wait_part(row, part, stage):
        remote(
            arrived.at[stage, row, part],
            arrived.at[stage, row, part],
            send_sem.at[stage, 0, 0],
            recv_sem.at[stage, row, part],
            mate,
        ).wait_recv()

    def hand_on(row, stage):
        kind, number = rows[row]
        wait_part(row, core, stage)
        mate_copy(row, stage).start()
        if kind == "heavy" and number < e_lanes:
            cross_copy(row, stage).start()

    def products(value, left, right):
        re_high, re_low = split(value[0])
        im_high, im_low = split(value[1])
        column = jnp.concatenate(
            [
                jnp.concatenate([re_high, re_low, re_high], axis=0),
                jnp.concatenate([im_high, im_low, im_high], axis=0),
            ],
            axis=1,
        )
        row = jnp.concatenate(
            [
                jnp.concatenate([re_high, re_low, re_high], axis=1),
                jnp.concatenate([im_high, im_low, im_high], axis=1),
            ],
            axis=0,
        )
        p = jnp.dot(left, column, preferred_element_type=F32)
        r = jnp.dot(row, right, preferred_element_type=F32)
        return p[:, :order], p[:, order:], r[:order], r[order:]

    def add_row(code, value, scale, stage):
        weight, target, mode, occ = code & 1, get(TARGET, code), get(MODE, code), get(OCC, code)
        lower = get(FLAG, code) == 1
        a = jnp.where(lower, F32(1.0), bath_ref[0, mode])
        b = jnp.where(lower, F32(0.0), bath_ref[1, mode])
        p_re, p_im, r_re, r_im = products(value, op_left[mode], op_right[mode])
        root = jnp.sqrt(jnp.full((1, order), occ, I32).astype(F32)) * weight.astype(F32) * scale
        ca = root * a
        cb = root * b
        term_ref[0] = ca * (p_im - r_im) + cb * (p_re + r_re)
        term_ref[1] = cb * (p_im + r_im) - ca * (p_re - r_re)

        def add_to(acc):
            def add(s, carry):
                chosen = jnp.where(target == s, F32(1.0), F32(0.0))
                acc[s] = acc[s] + chosen * term_ref[...]
                return carry

            lax.fori_loop(0, mats, add, 0)

        pl.when(stage == 0)(functools.partial(add_to, state.at[1]))
        pl.when(stage == 1)(functools.partial(add_to, out_ref))

    def prepare_operators():
        loads[1].wait()
        loads[2].wait()

        def prepare(k, carry):
            high, low = split(coup_ref[k])
            op_left[k] = jnp.concatenate([high, high, low], axis=1)
            op_right[k] = jnp.concatenate([high, high, low], axis=0)
            return carry

        lax.fori_loop(0, modes, prepare, 0)
        high, low = split(ham_ref[...])
        op_left[modes] = jnp.concatenate([high, high, low], axis=1)
        op_right[modes] = jnp.concatenate([high, high, low], axis=0)

    half_square = F32(0.5 * STEP * STEP)

    def stage_rows(stage, carry):
        source = state.at[stage]
        scale = jnp.where(stage == 0, F32(1.0), half_square)
        shares = share_copies(source, stage)

        for n in range(len(direct)):
            packed[n] = source[match_ref[direct[n], 0]]
            if n > 0:
                direct_copy(n - 1, stage, 0).start()
            if n == 1:
                shares[0].start()
        for part in range(2):
            direct_copy(len(direct) - 1, stage, part).start()
        shares[1].start()

        @pl.when(stage == 0)
        def _():
            prepare_operators()

        def own(n, carry):
            value = source[n]
            p_re, p_im, r_re, r_im = products(value, op_left[modes], op_right[modes])
            slope_re = (p_im - r_im) - damp_ref[n] * value[0]
            slope_im = (r_re - p_re) - damp_ref[n] * value[1]

            @pl.when(stage == 0)
            def _():
                state[1, n, 0] = slope_re
                state[1, n, 1] = slope_im

            @pl.when(stage == 1)
            def _():
                out_ref[n, 0] = state[0, n, 0] + F32(STEP) * value[0] + half_square * slope_re
                out_ref[n, 1] = state[0, n, 1] + F32(STEP) * value[1] + half_square * slope_im

            return carry

        lax.fori_loop(0, mats, own, 0)

        shares[0].wait_recv()
        tables = {"level": level_ref, "heavy": heavy_ref, "light": light_ref}
        for n, (kind, number) in enumerate(outgoing):
            code = tables[kind][(me // 2) * WIDTH + number]
            slot = get(SLOT, code)
            lanes[n] = jnp.where(get(CORE, code) == core, source[slot, core], share_mine[stage, slot])
            if n > 0:
                when(leaves(n - 1))(lane_copy(n - 1, stage).start)
        when(leaves(len(outgoing) - 1))(lane_copy(len(outgoing) - 1, stage).start)
        for n in range(len(direct) - 1):
            direct_copy(n, stage, 1).start()

        shares[1].wait_recv()

        def near_row(i, carry):
            code = fact[near + i]
            slot = get(SLOT, code)
            my_part = share_mine[stage, slot]
            other_part = share_other[stage, slot]
            is_real = core == 0
            value = (jnp.where(is_real, my_part, other_part), jnp.where(is_real, other_part, my_part))
            add_row(code, value, scale, stage)
            return carry

        lax.fori_loop(0, 2, near_row, 0)

        def row_step(i, carry):
            there = i >= 0
            is_lane = i < 0
            for row in lane_rows:
                used = lands(row)
                now = i == max(row - 2, 0)
                when(now if used is None else now & used)(functools.partial(hand_on, row, stage))
                is_lane = is_lane | (i == row)
                if used is not None:
                    there = there & ((i != row) | used)

            @pl.when(there)
            def _():
                wait_part(i, 1 - core, stage)

                @pl.when(jnp.logical_not(is_lane))
                def _():
                    wait_part(i, core, stage)

                add_row(fact[i], arrived[stage, i], scale, stage)

            return carry

        lax.fori_loop(0, len(rows), row_step, 0)

        for share in shares:
            share.wait_send()
        for n in range(len(direct)):
            for part in range(2):
                direct_copy(n, stage, part).wait_send()
        for n in range(len(outgoing)):
            when(leaves(n))(lane_copy(n, stage).wait_send)
        for row in lane_rows:
            kind, number = rows[row]

            def sent():
                mate_copy(row, stage).wait_send()
                if kind == "heavy" and number < e_lanes:
                    cross_copy(row, stage).wait_send()

            when(lands(row))(sent)
        return carry

    loads[0].wait()
    lax.fori_loop(0, 2, stage_rows, 0)


def body(tier_size, rho, hamiltonian, couplings, bath_coef, damping, match_edges, left_rows, left_count):
    mats, _, order, _ = rho.shape
    modes = couplings.shape[0]
    table = match_edges.reshape(-1, match_edges.shape[-1])
    colours = table.shape[0]
    vmem = pl.BlockSpec(memory_space=pltpu.VMEM)
    hbm = pl.BlockSpec(memory_space=pl.ANY)
    smem = pl.BlockSpec(memory_space=pltpu.SMEM)

    pair, heavy, light, level, pick = pl.pallas_call(
        functools.partial(plan_kernel, tier_size, mats),
        out_shape=[
            jax.ShapeDtypeStruct((tier_size * 2 * REACH + 1,), I32),
            jax.ShapeDtypeStruct((tier_size // 2 * WIDTH,), I32),
            jax.ShapeDtypeStruct((tier_size // 2 * WIDTH,), I32),
            jax.ShapeDtypeStruct((tier_size // 2 * WIDTH,), I32),
            jax.ShapeDtypeStruct((1,), I32),
        ],
        in_specs=[smem, smem],
        out_specs=[smem] * 5,
    )(left_rows.transpose(2, 1, 0), left_count)

    def step(number, variant):
        order_of_rows = row_order(variant, colours)
        rows = len(order_of_rows)
        lanes = sum(kind in ("level", "heavy", "light") for kind, _ in order_of_rows)
        direct = colours - 1
        return pl.pallas_call(
            functools.partial(kernel, tier_size, colours, variant),
            out_shape=pltpu.VMEM(rho.shape, F32),
            in_specs=[hbm, hbm, hbm] + [smem] * 7,
            out_specs=vmem,
            scratch_shapes=[
                pltpu.VMEM((2,) + rho.shape, F32),
                pltpu.VMEM(hamiltonian.shape, F32),
                pltpu.VMEM(couplings.shape, F32),
                pltpu.SemaphoreType.DMA((3,)),
                pltpu.VMEM((2, order, order), F32),
                pltpu.VMEM((2, mats, order, order), F32),
                pltpu.VMEM((2, mats, order, order), F32),
                pltpu.VMEM((direct, 2, order, order), F32),
                pltpu.VMEM((lanes, order, order), F32),
                pltpu.VMEM((2, rows, 2, order, order), F32),
                pltpu.VMEM((modes + 1, order, 3 * order), BF16),
                pltpu.VMEM((modes + 1, 3 * order, order), BF16),
                pltpu.SMEM((rows + 2,), I32),
                pltpu.SemaphoreType.DMA((2, 2)),
                pltpu.SemaphoreType.DMA((2, 2)),
                pltpu.SemaphoreType.DMA((2, direct + rows, 3)),
                pltpu.SemaphoreType.DMA((2, rows, 2)),
            ],
            compiler_params=pltpu.CompilerParams(
                collective_id=number, has_side_effects=True, vmem_limit_bytes=58 * 1024 * 1024
            ),
        )

    return lax.switch(
        pick[0],
        [step(i, variant) for i, variant in enumerate(VARIANTS)],
        rho,
        hamiltonian,
        couplings,
        bath_coef.T,
        damping,
        table,
        pair,
        heavy,
        light,
        level,
    )


def solution(mesh):
    placed = (
        P(("groups", "tier"), None, None, None),
        P(),
        P(),
        P("groups", None),
        P(("groups", "tier")),
        P("tier", None, None, None),
        P(),
        P(),
    )
    return jax.shard_map(
        functools.partial(body, mesh.shape["tier"]),
        mesh=mesh,
        in_specs=placed,
        out_specs=P(("groups", "tier"), None, None, None),
        check_vma=False,
    )
```

```python
import functools

import jax
import jax.numpy as jnp
from jax import lax
from jax.experimental import pallas as pl
from jax.experimental.pallas import tpu as pltpu
from jax.sharding import PartitionSpec as P

REACH = 4
STEP = 0.1
F32 = jnp.float32
BF16 = jnp.bfloat16
I32 = jnp.int32

SLOT = (1, 63)
TARGET = (7, 63)
MODE = (13, 31)
FLAG = (18, 1)
OCC = (19, 15)
CORE = (23, 1)
PLACE = (24, 3)

HEAVY = ((2, 0), (2, 1), (3, 0), (3, 1), (2, 2), (3, 2), (3, 3))
LIGHT = ((2, 2), (2, 3), (3, 3))
CROSSING = 4
LEVEL = ((2, 0), (2, 1), (3, 0), (3, 1))
WIDTH = 8

VARIANTS = (
    (3, 2, 2, 1, 0, 2, 3),
    (2, 2, 2, 2, 1, 2, 3),
    (3, 2, 2, 1, 1, 2, 3),
    (3, 2, 3, 2, 1, 2, 3),
    (2, 3, 2, 3, 2, 2, 3),
    (4, 2, 4, 2, 0, 3, 4),
    (4, 3, 4, 3, 1, 3, 4),
    (7, 3, 7, 3, 0, 4, 4),
)


def split(value):
    high = value.astype(BF16)
    low = (value - high.astype(F32)).astype(BF16)
    return high, low


def flip(index, stride):
    return index + stride - 2 * stride * ((index // stride) % 2)


def put(field, value):
    return value << field[0]


def get(field, code):
    return (code >> field[0]) & field[1]


def distance_index(source, target, tier_size):
    d = lax.rem(source - target + tier_size, tier_size)
    return jnp.where(d <= REACH, d - 1, d - tier_size + 2 * REACH)


def plan_kernel(tier_size, mats, left_ref, count_ref, pair_ref, heavy_ref, light_ref, level_ref, count_out, pick_ref):
    left_cap = left_ref.shape[1]
    places = 2 * REACH
    planes = tier_size // REACH

    for ref in (pair_ref, heavy_ref, light_ref, level_ref):
        for i in range(ref.shape[0]):
            ref[i] = jnp.int32(0)

    for b in range(tier_size):
        count = count_ref[b]
        for j in range(left_cap):
            source = left_ref[1, j, b]
            owner = lax.div(source, jnp.int32(mats))
            code = 1 + put(SLOT, source - owner * mats) + put(TARGET, left_ref[0, j, b])
            code = code + put(MODE, left_ref[2, j, b]) + put(FLAG, left_ref[3, j, b]) + put(OCC, left_ref[4, j, b])
            index = jnp.clip(distance_index(owner, b, tier_size), 0, places - 1)
            pair_ref[jnp.where(j < count, b * places + index, tier_size * places)] = code

    found = {}
    for k in range(tier_size // 2):
        plane, half = k // 2, k % 2
        toward = 2 * half - 1

        def place(m):
            return m if half == 1 else REACH - 1 - m

        def fill(ref, pairs, other):
            rank = jnp.int32(k * WIDTH)
            ranks = []
            for m_source, m_target in pairs:
                source = plane * REACH + place(m_source)
                target = other % planes * REACH + place(m_target)
                d = (source - target) % tier_size
                index = d - 1 if d <= REACH else d - tier_size + places
                code = pair_ref[target * places + index]
                ref[rank] = code + ((source % 2) << CORE[0]) + (place(m_target) << PLACE[0])
                rank = rank + (code & 1)
                ranks.append(rank - k * WIDTH)
            ref[rank] = jnp.int32(0)
            return ranks

        heavy = fill(heavy_ref, HEAVY, plane + toward)
        light = fill(light_ref, LIGHT, plane - toward)
        level = fill(level_ref, LEVEL, plane)
        count_out[k] = heavy[-1]
        wraps = not 0 <= plane + toward < planes
        found[k] = (wraps, heavy[-1], heavy[CROSSING - 1], light[-1], level[-1])

    pick = jnp.int32(len(VARIANTS) - 1)
    for i in reversed(range(len(VARIANTS) - 1)):
        a, b, a_wrap, b_wrap, o, e, f = VARIANTS[i]
        fits = None
        for k in found:
            wraps, heavy, crossing, _, level = found[k]
            light = found[k + 1 - 2 * (k % 2)][3]
            spill = jnp.maximum(heavy - (a_wrap if wraps else a), 0)
            fit = (spill <= jnp.minimum(crossing, o)) & (light + spill <= (b_wrap if wraps else b))
            fit = fit & (crossing - spill <= e) & (level <= f)
            fits = fit if fits is None else fits & fit
        pick = jnp.where(fits, i, pick)
    pick_ref[0] = pick


def row_order(variant, colours):
    a, b, a_wrap, b_wrap, o, e, f = variant
    timed = [(0.6 + i, 0, "level", i) for i in range(f)]
    timed += [(1.0 + i, 1, "heavy", i) for i in range(max(a, a_wrap))]
    late = min(b, b_wrap) - o
    timed += [(1.2 + i + (1.5 if i >= late else 0.0), 2, "light", i) for i in range(max(b, b_wrap))]
    timed += [(3.1 + i, 3, "cross", i) for i in range(e)]
    lanes = [(kind, i) for _, _, kind, i in sorted(timed)]
    return [("colour", 1)] + lanes + [("colour", c) for c in range(colours - 1, 1, -1)]


def kernel(
    tier_size,
    colours,
    variant,
    rho_any,
    ham_any,
    coup_any,
    bath_ref,
    damp_ref,
    match_ref,
    pair_ref,
    heavy_ref,
    light_ref,
    level_ref,
    heavy_count,
    out_ref,
    state,
    ham_ref,
    coup_ref,
    load_sem,
    term_ref,
    share_mine,
    share_other,
    packed,
    lanes,
    spill_out,
    spill_in,
    arrived,
    op_left,
    op_right,
    fact,
    share_send,
    share_recv,
    spill_send,
    spill_recv,
    send_sem,
    recv_sem,
):
    loads = [
        pltpu.make_async_copy(rho_any, state.at[0], load_sem.at[0]),
        pltpu.make_async_copy(ham_any, ham_ref, load_sem.at[1]),
        pltpu.make_async_copy(coup_any, coup_ref, load_sem.at[2]),
    ]
    for load in loads:
        load.start()
    me = lax.axis_index("tier")
    mats = rho_any.shape[0]
    order = rho_any.shape[2]
    modes = coup_ref.shape[0]
    places = 2 * REACH
    a_lanes, b_lanes, a_wrap, b_wrap, spills, e_lanes, _ = variant
    rows = row_order(variant, colours)
    index_of = {row: i for i, row in enumerate(rows)}
    lane_rows = [i for i, (kind, _) in enumerate(rows) if kind != "colour"]

    core = me % 2
    place = me % REACH
    half = place // 2
    toward = 2 * half - 1
    mate = flip(me, 1)
    across = flip(me, 2)
    plane = me // REACH
    planes = tier_size // REACH
    heavy_to = lax.rem(me + REACH * toward + tier_size, tier_size)
    light_to = lax.rem(me - REACH * toward + tier_size, tier_size)
    partners = [flip(me, 2**c) for c in range(colours)]

    heavy_wraps = (plane + toward < 0) | (plane + toward >= planes)
    light_wraps = (plane - toward < 0) | (plane - toward >= planes)

    greeted = [mate, across, heavy_to, light_to] + partners[2:]
    barrier = pltpu.get_barrier_semaphore()
    for device in greeted:
        pl.semaphore_signal(barrier, inc=1, device_id={"tier": device}, device_id_type=pl.DeviceIdType.MESH)
    pl.semaphore_wait(barrier, len(greeted))

    def remote(source, target, send, recv, device):
        return pltpu.make_async_remote_copy(
            src_ref=source,
            dst_ref=target,
            send_sem=send,
            recv_sem=recv,
            device_id={"tier": device},
            device_id_type=pl.DeviceIdType.MESH,
        )

    def lane_used(kind, number, wraps):
        line, wrap = {"heavy": (a_lanes, a_wrap), "light": (b_lanes, b_wrap)}[kind]
        if number < min(line, wrap):
            return None
        return jnp.logical_not(wraps) if number < line else wraps

    def when(condition):
        if condition is None:
            return lambda run: run()
        return pl.when(condition)

    def lands(row):
        kind, number = rows[row]
        if kind == "heavy":
            return lane_used("heavy", number, light_wraps)
        if kind == "light":
            return lane_used("light", number, heavy_wraps)
        if kind == "cross":
            return lane_used("heavy", number, heavy_wraps)
        return None

    def pair_code(source, target):
        return pair_ref[target * places + distance_index(source, target, tier_size)]

    def match_code(c):
        return (
            1
            + put(TARGET, match_ref[c, 0])
            + put(SLOT, match_ref[c, 1])
            + put(MODE, match_ref[c, 2])
            + put(FLAG, match_ref[c, 3])
            + put(OCC, match_ref[c, 4])
        )

    def mine(code):
        return jnp.where(get(PLACE, code) == place, code, 0)

    def spilt(chip, wraps):
        return jnp.clip(heavy_count[chip] - jnp.where(wraps, a_wrap, a_lanes), 0, spills)

    def heavy_code(chip, wraps, number):
        if not spills:
            return heavy_ref[chip * WIDTH + number]
        return heavy_ref[chip * WIDTH + number + spilt(chip, wraps)]

    def spill_code(chip, wraps, number):
        return jnp.where(number < spilt(chip, wraps), heavy_ref[chip * WIDTH + number], 0)

    first_late = min(b_lanes, b_wrap) - spills

    def light_code(chip, other, wraps, number):
        own = light_ref[chip * WIDTH + number]
        if number < first_late:
            return own, None, None
        which = jnp.where(wraps, b_wrap, b_lanes) - 1 - number
        inside = jnp.clip(which, 0, max(spills - 1, 0))
        taken = (which >= 0) & (which < spilt(other, wraps))
        return jnp.where(taken, heavy_ref[other * WIDTH + inside], own), taken, inside

    heavy_from = light_to // 2
    light_from = heavy_to // 2
    cross_from = lax.rem(across + REACH * toward + tier_size, tier_size) // 2
    for i, (kind, number) in enumerate(rows):
        if kind == "colour":
            fact[i] = match_code(number)
        elif kind == "level":
            fact[i] = mine(level_ref[(across // 2) * WIDTH + number])
        elif kind == "heavy":
            fact[i] = mine(heavy_code(heavy_from, light_wraps, number))
        elif kind == "light":
            fact[i] = mine(light_code(light_from, cross_from, heavy_wraps, number)[0])
        else:
            fact[i] = mine(heavy_code(cross_from, heavy_wraps, number))
    near = len(rows)
    fact[near] = match_code(0)
    fact[near + 1] = pair_code(mate, me)

    direct = list(range(colours - 1, 0, -1))

    def direct_copy(n, stage, part):
        row = index_of[("colour", direct[n])]
        return remote(
            packed.at[n, part],
            arrived.at[stage, row, part],
            send_sem.at[stage, n, part],
            recv_sem.at[stage, row, part],
            partners[direct[n]],
        )

    outgoing = [row for row in rows if row[0] in ("level", "heavy", "light")]

    def leaves(n):
        kind, number = outgoing[n]
        if kind == "level":
            return None
        return lane_used(kind, number, heavy_wraps if kind == "heavy" else light_wraps)

    def spill_copy(n, stage):
        return remote(
            spill_out.at[n],
            spill_in.at[stage, n],
            spill_send.at[stage, n],
            spill_recv.at[stage, n],
            across,
        )

    def lane_copy(n, stage):
        row = index_of[outgoing[n]]
        return remote(
            lanes.at[n],
            arrived.at[stage, row, core],
            send_sem.at[stage, len(direct) + n, 0],
            recv_sem.at[stage, row, core],
            {"level": across, "heavy": heavy_to, "light": light_to}[outgoing[n][0]],
        )

    def mate_copy(row, stage):
        return remote(
            arrived.at[stage, row, core],
            arrived.at[stage, row, core],
            send_sem.at[stage, len(direct) + row, 1],
            recv_sem.at[stage, row, core],
            mate,
        )

    def cross_copy(row, stage):
        landing = index_of[("cross", rows[row][1])]
        return remote(
            arrived.at[stage, row, core],
            arrived.at[stage, landing, core],
            send_sem.at[stage, len(direct) + row, 2],
            recv_sem.at[stage, landing, core],
            across,
        )

    def share_copies(source, stage):
        return [
            remote(source.at[:, 1 - core], share_mine.at[stage], share_send.at[stage, 0], share_recv.at[stage, 0], mate),
            remote(source.at[:, core], share_other.at[stage], share_send.at[stage, 1], share_recv.at[stage, 1], mate),
        ]

    def wait_part(row, part, stage):
        remote(
            arrived.at[stage, row, part],
            arrived.at[stage, row, part],
            send_sem.at[stage, 0, 0],
            recv_sem.at[stage, row, part],
            mate,
        ).wait_recv()

    def hand_on(row, stage):
        kind, number = rows[row]
        wait_part(row, core, stage)
        mate_copy(row, stage).start()
        if kind == "heavy" and number < e_lanes:
            cross_copy(row, stage).start()

    def products(value, left, right):
        re_high, re_low = split(value[0])
        im_high, im_low = split(value[1])
        column = jnp.concatenate(
            [
                jnp.concatenate([re_high, re_low, re_high], axis=0),
                jnp.concatenate([im_high, im_low, im_high], axis=0),
            ],
            axis=1,
        )
        row = jnp.concatenate(
            [
                jnp.concatenate([re_high, re_low, re_high], axis=1),
                jnp.concatenate([im_high, im_low, im_high], axis=1),
            ],
            axis=0,
        )
        p = jnp.dot(left, column, preferred_element_type=F32)
        r = jnp.dot(row, right, preferred_element_type=F32)
        return p[:, :order], p[:, order:], r[:order], r[order:]

    def add_row(code, value, scale, stage):
        weight, target, mode, occ = code & 1, get(TARGET, code), get(MODE, code), get(OCC, code)
        lower = get(FLAG, code) == 1
        a = jnp.where(lower, F32(1.0), bath_ref[0, mode])
        b = jnp.where(lower, F32(0.0), bath_ref[1, mode])
        p_re, p_im, r_re, r_im = products(value, op_left[mode], op_right[mode])
        root = jnp.sqrt(jnp.full((1, order), occ, I32).astype(F32)) * weight.astype(F32) * scale
        ca = root * a
        cb = root * b
        term_ref[0] = ca * (p_im - r_im) + cb * (p_re + r_re)
        term_ref[1] = cb * (p_im + r_im) - ca * (p_re - r_re)

        def add_to(acc):
            def add(s, carry):
                chosen = jnp.where(target == s, F32(1.0), F32(0.0))
                acc[s] = acc[s] + chosen * term_ref[...]
                return carry

            lax.fori_loop(0, mats, add, 0)

        pl.when(stage == 0)(functools.partial(add_to, state.at[1]))
        pl.when(stage == 1)(functools.partial(add_to, out_ref))

    def prepare_operators():
        loads[1].wait()
        loads[2].wait()

        def prepare(k, carry):
            high, low = split(coup_ref[k])
            op_left[k] = jnp.concatenate([high, high, low], axis=1)
            op_right[k] = jnp.concatenate([high, high, low], axis=0)
            return carry

        lax.fori_loop(0, modes, prepare, 0)
        high, low = split(ham_ref[...])
        op_left[modes] = jnp.concatenate([high, high, low], axis=1)
        op_right[modes] = jnp.concatenate([high, high, low], axis=0)

    half_square = F32(0.5 * STEP * STEP)

    def stage_rows(stage, carry):
        source = state.at[stage]
        scale = jnp.where(stage == 0, F32(1.0), half_square)
        shares = share_copies(source, stage)

        for n in range(len(direct)):
            packed[n] = source[match_ref[direct[n], 0]]
            if n > 0:
                direct_copy(n - 1, stage, 0).start()
            if n == 1:
                shares[0].start()
        direct_copy(len(direct) - 1, stage, 0).start()
        shares[1].start()

        @pl.when(stage == 0)
        def _():
            prepare_operators()

        def own(n, carry):
            value = source[n]
            p_re, p_im, r_re, r_im = products(value, op_left[modes], op_right[modes])
            slope_re = (p_im - r_im) - damp_ref[n] * value[0]
            slope_im = (r_re - p_re) - damp_ref[n] * value[1]

            @pl.when(stage == 0)
            def _():
                state[1, n, 0] = slope_re
                state[1, n, 1] = slope_im

            @pl.when(stage == 1)
            def _():
                out_ref[n, 0] = state[0, n, 0] + F32(STEP) * value[0] + half_square * slope_re
                out_ref[n, 1] = state[0, n, 1] + F32(STEP) * value[1] + half_square * slope_im

            return carry

        lax.fori_loop(0, mats // 2, own, 0)

        shares[0].wait_recv()
        chip, other = me // 2, across // 2

        def chosen(code):
            slot = get(SLOT, code)
            return jnp.where(get(CORE, code) == core, source[slot, core], share_mine[stage, slot])

        for n in range(spills):
            spill_out[n] = chosen(spill_code(chip, heavy_wraps, n))
            if n > 0:
                spill_copy(n - 1, stage).start()

        def is_late(n):
            return outgoing[n][0] == "light" and outgoing[n][1] >= first_late

        early = [n for n in range(len(outgoing)) if not is_late(n)]
        late = [n for n in range(len(outgoing)) if is_late(n)]
        for turn, n in enumerate(early):
            kind, number = outgoing[n]
            if kind == "level":
                code = level_ref[chip * WIDTH + number]
            elif kind == "heavy":
                code = heavy_code(chip, heavy_wraps, number)
            else:
                code = light_code(chip, other, light_wraps, number)[0]
            lanes[n] = chosen(code)
            if turn > 0:
                before = early[turn - 1]
                when(leaves(before))(lane_copy(before, stage).start)
            else:
                if spills:
                    spill_copy(spills - 1, stage).start()
                direct_copy(len(direct) - 1, stage, 1).start()
        when(leaves(early[-1]))(lane_copy(early[-1], stage).start)

        lax.fori_loop(mats // 2, mats, own, 0)
        shares[1].wait_recv()

        def near_row(i, carry):
            code = fact[near + i]
            slot = get(SLOT, code)
            my_part = share_mine[stage, slot]
            other_part = share_other[stage, slot]
            is_real = core == 0
            value = (jnp.where(is_real, my_part, other_part), jnp.where(is_real, other_part, my_part))
            add_row(code, value, scale, stage)
            return carry

        lax.fori_loop(0, 2, near_row, 0)

        for n in range(spills):
            spill_copy(n, stage).wait_recv()
        for n in late:
            code, taken, inside = light_code(chip, other, light_wraps, outgoing[n][1])
            value = chosen(code)
            if spills:
                value = jnp.where(taken, spill_in[stage, inside], value)
            lanes[n] = value
        for n in late:
            when(leaves(n))(lane_copy(n, stage).start)
        for n in range(len(direct) - 1):
            direct_copy(n, stage, 1).start()

        def row_step(i, carry):
            there = i >= 0
            is_lane = i < 0
            for row in lane_rows:
                used = lands(row)
                now = i == max(row - 2, 0)
                when(now if used is None else now & used)(functools.partial(hand_on, row, stage))
                is_lane = is_lane | (i == row)
                if used is not None:
                    there = there & ((i != row) | used)

            @pl.when(there)
            def _():
                wait_part(i, 1 - core, stage)

                @pl.when(jnp.logical_not(is_lane))
                def _():
                    wait_part(i, core, stage)

                add_row(fact[i], arrived[stage, i], scale, stage)

            return carry

        lax.fori_loop(0, len(rows), row_step, 0)

        for share in shares:
            share.wait_send()
        for n in range(spills):
            spill_copy(n, stage).wait_send()
        for n in range(len(direct)):
            for part in range(2):
                direct_copy(n, stage, part).wait_send()
        for n in range(len(outgoing)):
            when(leaves(n))(lane_copy(n, stage).wait_send)
        for row in lane_rows:
            kind, number = rows[row]

            def sent():
                mate_copy(row, stage).wait_send()
                if kind == "heavy" and number < e_lanes:
                    cross_copy(row, stage).wait_send()

            when(lands(row))(sent)
        return carry

    loads[0].wait()
    lax.fori_loop(0, 2, stage_rows, 0)


def body(tier_size, rho, hamiltonian, couplings, bath_coef, damping, match_edges, left_rows, left_count):
    mats, _, order, _ = rho.shape
    modes = couplings.shape[0]
    table = match_edges.reshape(-1, match_edges.shape[-1])
    colours = table.shape[0]
    vmem = pl.BlockSpec(memory_space=pltpu.VMEM)
    hbm = pl.BlockSpec(memory_space=pl.ANY)
    smem = pl.BlockSpec(memory_space=pltpu.SMEM)

    pair, heavy, light, level, count, pick = pl.pallas_call(
        functools.partial(plan_kernel, tier_size, mats),
        out_shape=[
            jax.ShapeDtypeStruct((tier_size * 2 * REACH + 1,), I32),
            jax.ShapeDtypeStruct((tier_size // 2 * WIDTH,), I32),
            jax.ShapeDtypeStruct((tier_size // 2 * WIDTH,), I32),
            jax.ShapeDtypeStruct((tier_size // 2 * WIDTH,), I32),
            jax.ShapeDtypeStruct((tier_size // 2,), I32),
            jax.ShapeDtypeStruct((1,), I32),
        ],
        in_specs=[smem, smem],
        out_specs=[smem] * 6,
    )(left_rows.transpose(2, 1, 0), left_count)

    def step(number, variant):
        order_of_rows = row_order(variant, colours)
        rows = len(order_of_rows)
        lanes = sum(kind in ("level", "heavy", "light") for kind, _ in order_of_rows)
        direct = colours - 1
        spills = max(variant[4], 1)
        return pl.pallas_call(
            functools.partial(kernel, tier_size, colours, variant),
            out_shape=pltpu.VMEM(rho.shape, F32),
            in_specs=[hbm, hbm, hbm] + [smem] * 8,
            out_specs=vmem,
            scratch_shapes=[
                pltpu.VMEM((2,) + rho.shape, F32),
                pltpu.VMEM(hamiltonian.shape, F32),
                pltpu.VMEM(couplings.shape, F32),
                pltpu.SemaphoreType.DMA((3,)),
                pltpu.VMEM((2, order, order), F32),
                pltpu.VMEM((2, mats, order, order), F32),
                pltpu.VMEM((2, mats, order, order), F32),
                pltpu.VMEM((direct, 2, order, order), F32),
                pltpu.VMEM((lanes, order, order), F32),
                pltpu.VMEM((spills, order, order), F32),
                pltpu.VMEM((2, spills, order, order), F32),
                pltpu.VMEM((2, rows, 2, order, order), F32),
                pltpu.VMEM((modes + 1, order, 3 * order), BF16),
                pltpu.VMEM((modes + 1, 3 * order, order), BF16),
                pltpu.SMEM((rows + 2,), I32),
                pltpu.SemaphoreType.DMA((2, 2)),
                pltpu.SemaphoreType.DMA((2, 2)),
                pltpu.SemaphoreType.DMA((2, spills)),
                pltpu.SemaphoreType.DMA((2, spills)),
                pltpu.SemaphoreType.DMA((2, direct + rows, 3)),
                pltpu.SemaphoreType.DMA((2, rows, 2)),
            ],
            compiler_params=pltpu.CompilerParams(
                collective_id=number, has_side_effects=True, vmem_limit_bytes=58 * 1024 * 1024
            ),
        )

    return lax.switch(
        pick[0],
        [step(i, variant) for i, variant in enumerate(VARIANTS)],
        rho,
        hamiltonian,
        couplings,
        bath_coef.T,
        damping,
        table,
        pair,
        heavy,
        light,
        level,
        count,
    )


def solution(mesh):
    placed = (
        P(("groups", "tier"), None, None, None),
        P(),
        P(),
        P("groups", None),
        P(("groups", "tier")),
        P("tier", None, None, None),
        P(),
        P(),
    )
    return jax.shard_map(
        functools.partial(body, mesh.shape["tier"]),
        mesh=mesh,
        in_specs=placed,
        out_specs=P(("groups", "tier"), None, None, None),
        check_vma=False,
    )
```

```python
import functools

import jax
import jax.numpy as jnp
from jax import lax
from jax.experimental import pallas as pl
from jax.experimental.pallas import tpu as pltpu
from jax.sharding import PartitionSpec as P

REACH = 4
STEP = 0.1
F32 = jnp.float32
BF16 = jnp.bfloat16
I32 = jnp.int32

SLOT = (1, 63)
TARGET = (7, 63)
MODE = (13, 31)
FLAG = (18, 1)
OCC = (19, 15)
CORE = (23, 1)
PLACE = (24, 3)

HEAVY = ((2, 0), (2, 1), (3, 0), (3, 1), (2, 2), (3, 2), (3, 3))
LIGHT = ((2, 2), (2, 3), (3, 3))
CROSSING = 4
LEVEL = ((2, 0), (2, 1), (3, 0), (3, 1))
WIDTH = 8

VARIANTS = (
    (3, 2, 2, 1, 0, 3, 3),
    (2, 2, 2, 2, 1, 2, 3),
    (3, 3, 2, 2, 2, 2, 3),
    (2, 3, 2, 3, 2, 2, 3),
    (4, 3, 3, 2, 2, 3, 3),
    (3, 2, 4, 3, 1, 3, 4),
    (3, 3, 3, 3, 2, 2, 4),
    (7, 3, 7, 3, 0, 4, 4),
)


def split(value):
    high = value.astype(BF16)
    low = (value - high.astype(F32)).astype(BF16)
    return high, low


def flip(index, stride):
    return index + stride - 2 * stride * ((index // stride) % 2)


def put(field, value):
    return value << field[0]


def get(field, code):
    return (code >> field[0]) & field[1]


def distance_index(source, target, tier_size):
    d = lax.rem(source - target + tier_size, tier_size)
    return jnp.where(d <= REACH, d - 1, d - tier_size + 2 * REACH)


def plan_kernel(tier_size, mats, left_ref, count_ref, pair_ref, heavy_ref, light_ref, level_ref, count_out, pick_ref):
    left_cap = left_ref.shape[1]
    places = 2 * REACH
    planes = tier_size // REACH

    for ref in (pair_ref, heavy_ref, light_ref, level_ref):
        for i in range(ref.shape[0]):
            ref[i] = jnp.int32(0)

    for b in range(tier_size):
        count = count_ref[b]
        for j in range(left_cap):
            source = left_ref[1, j, b]
            owner = lax.div(source, jnp.int32(mats))
            code = 1 + put(SLOT, source - owner * mats) + put(TARGET, left_ref[0, j, b])
            code = code + put(MODE, left_ref[2, j, b]) + put(FLAG, left_ref[3, j, b]) + put(OCC, left_ref[4, j, b])
            index = jnp.clip(distance_index(owner, b, tier_size), 0, places - 1)
            pair_ref[jnp.where(j < count, b * places + index, tier_size * places)] = code

    found = {}
    for k in range(tier_size // 2):
        plane, half = k // 2, k % 2
        toward = 2 * half - 1

        def place(m):
            return m if half == 1 else REACH - 1 - m

        def fill(ref, pairs, other):
            rank = jnp.int32(k * WIDTH)
            ranks = []
            for m_source, m_target in pairs:
                source = plane * REACH + place(m_source)
                target = other % planes * REACH + place(m_target)
                d = (source - target) % tier_size
                index = d - 1 if d <= REACH else d - tier_size + places
                code = pair_ref[target * places + index]
                ref[rank] = code + ((source % 2) << CORE[0]) + (place(m_target) << PLACE[0])
                rank = rank + (code & 1)
                ranks.append(rank - k * WIDTH)
            ref[rank] = jnp.int32(0)
            return ranks

        heavy = fill(heavy_ref, HEAVY, plane + toward)
        light = fill(light_ref, LIGHT, plane - toward)
        level = fill(level_ref, LEVEL, plane)
        count_out[k] = heavy[-1]
        wraps = not 0 <= plane + toward < planes
        found[k] = (wraps, heavy[-1], heavy[CROSSING - 1], light[-1], level[-1])

    pick = jnp.int32(len(VARIANTS) - 1)
    for i in reversed(range(len(VARIANTS) - 1)):
        a, b, a_wrap, b_wrap, o, e, f = VARIANTS[i]
        fits = None
        for k in found:
            wraps, heavy, crossing, _, level = found[k]
            light = found[k + 1 - 2 * (k % 2)][3]
            spill = jnp.maximum(heavy - (a_wrap if wraps else a), 0)
            fit = (spill <= jnp.minimum(crossing, o)) & (light + spill <= (b_wrap if wraps else b))
            fit = fit & (crossing - spill <= e) & (level <= f)
            fits = fit if fits is None else fits & fit
        pick = jnp.where(fits, i, pick)
    pick_ref[0] = pick


def row_order(variant, colours):
    a, b, a_wrap, b_wrap, o, e, f = variant
    timed = [(0.6 + i, 0, "level", i) for i in range(f)]
    timed += [(1.0 + i, 1, "heavy", i) for i in range(max(a, a_wrap))]
    late = min(b, b_wrap) - o
    timed += [(1.2 + i + (1.5 if i >= late else 0.0), 2, "light", i) for i in range(max(b, b_wrap))]
    timed += [(3.1 + i, 3, "cross", i) for i in range(e)]
    lanes = [(kind, i) for _, _, kind, i in sorted(timed)]
    return [("colour", 1)] + lanes + [("colour", c) for c in range(colours - 1, 1, -1)]


def kernel(
    tier_size,
    colours,
    variant,
    rho_any,
    ham_any,
    coup_any,
    bath_ref,
    damp_ref,
    match_ref,
    pair_ref,
    heavy_ref,
    light_ref,
    level_ref,
    heavy_count,
    out_ref,
    state,
    ham_ref,
    coup_ref,
    load_sem,
    term_ref,
    share_mine,
    share_other,
    packed,
    lanes,
    spill_out,
    spill_in,
    arrived,
    op_left,
    op_right,
    fact,
    share_send,
    share_recv,
    spill_send,
    spill_recv,
    send_sem,
    recv_sem,
):
    loads = [
        pltpu.make_async_copy(rho_any, state.at[0], load_sem.at[0]),
        pltpu.make_async_copy(ham_any, ham_ref, load_sem.at[1]),
        pltpu.make_async_copy(coup_any, coup_ref, load_sem.at[2]),
    ]
    for load in loads:
        load.start()
    me = lax.axis_index("tier")
    mats = rho_any.shape[0]
    order = rho_any.shape[2]
    modes = coup_ref.shape[0]
    places = 2 * REACH
    a_lanes, b_lanes, a_wrap, b_wrap, spills, e_lanes, _ = variant
    rows = row_order(variant, colours)
    index_of = {row: i for i, row in enumerate(rows)}
    lane_rows = [i for i, (kind, _) in enumerate(rows) if kind != "colour"]

    core = me % 2
    place = me % REACH
    half = place // 2
    toward = 2 * half - 1
    mate = flip(me, 1)
    across = flip(me, 2)
    plane = me // REACH
    planes = tier_size // REACH
    heavy_to = lax.rem(me + REACH * toward + tier_size, tier_size)
    light_to = lax.rem(me - REACH * toward + tier_size, tier_size)
    partners = [flip(me, 2**c) for c in range(colours)]

    heavy_wraps = (plane + toward < 0) | (plane + toward >= planes)
    light_wraps = (plane - toward < 0) | (plane - toward >= planes)

    greeted = [mate, across, heavy_to, light_to] + partners[2:]
    barrier = pltpu.get_barrier_semaphore()
    for device in greeted:
        pl.semaphore_signal(barrier, inc=1, device_id={"tier": device}, device_id_type=pl.DeviceIdType.MESH)
    pl.semaphore_wait(barrier, len(greeted))

    def remote(source, target, send, recv, device):
        return pltpu.make_async_remote_copy(
            src_ref=source,
            dst_ref=target,
            send_sem=send,
            recv_sem=recv,
            device_id={"tier": device},
            device_id_type=pl.DeviceIdType.MESH,
        )

    def lane_used(kind, number, wraps):
        line, wrap = {"heavy": (a_lanes, a_wrap), "light": (b_lanes, b_wrap)}[kind]
        if number < min(line, wrap):
            return None
        return jnp.logical_not(wraps) if number < line else wraps

    def when(condition):
        if condition is None:
            return lambda run: run()
        return pl.when(condition)

    def lands(row):
        kind, number = rows[row]
        if kind == "heavy":
            return lane_used("heavy", number, light_wraps)
        if kind == "light":
            return lane_used("light", number, heavy_wraps)
        if kind == "cross":
            return lane_used("heavy", number, heavy_wraps)
        return None

    def pair_code(source, target):
        return pair_ref[target * places + distance_index(source, target, tier_size)]

    def match_code(c):
        return (
            1
            + put(TARGET, match_ref[c, 0])
            + put(SLOT, match_ref[c, 1])
            + put(MODE, match_ref[c, 2])
            + put(FLAG, match_ref[c, 3])
            + put(OCC, match_ref[c, 4])
        )

    def mine(code):
        return jnp.where(get(PLACE, code) == place, code, 0)

    def spilt(chip, wraps):
        return jnp.clip(heavy_count[chip] - jnp.where(wraps, a_wrap, a_lanes), 0, spills)

    def heavy_code(chip, wraps, number):
        if not spills:
            return heavy_ref[chip * WIDTH + number]
        return heavy_ref[chip * WIDTH + number + spilt(chip, wraps)]

    def spill_code(chip, wraps, number):
        return jnp.where(number < spilt(chip, wraps), heavy_ref[chip * WIDTH + number], 0)

    first_late = min(b_lanes, b_wrap) - spills

    def light_code(chip, other, wraps, number):
        own = light_ref[chip * WIDTH + number]
        if number < first_late:
            return own, None, None
        which = jnp.where(wraps, b_wrap, b_lanes) - 1 - number
        inside = jnp.clip(which, 0, max(spills - 1, 0))
        taken = (which >= 0) & (which < spilt(other, wraps))
        return jnp.where(taken, heavy_ref[other * WIDTH + inside], own), taken, inside

    heavy_from = light_to // 2
    light_from = heavy_to // 2
    cross_from = lax.rem(across + REACH * toward + tier_size, tier_size) // 2
    for i, (kind, number) in enumerate(rows):
        if kind == "colour":
            fact[i] = match_code(number)
        elif kind == "level":
            fact[i] = mine(level_ref[(across // 2) * WIDTH + number])
        elif kind == "heavy":
            fact[i] = mine(heavy_code(heavy_from, light_wraps, number))
        elif kind == "light":
            fact[i] = mine(light_code(light_from, cross_from, heavy_wraps, number)[0])
        else:
            fact[i] = mine(heavy_code(cross_from, heavy_wraps, number))
    near = len(rows)
    fact[near] = match_code(0)
    fact[near + 1] = pair_code(mate, me)

    direct = list(range(colours - 1, 0, -1))

    def direct_copy(n, stage, part):
        row = index_of[("colour", direct[n])]
        return remote(
            packed.at[n, part],
            arrived.at[stage, row, part],
            send_sem.at[stage, n, part],
            recv_sem.at[stage, row, part],
            partners[direct[n]],
        )

    outgoing = [row for row in rows if row[0] in ("level", "heavy", "light")]

    def leaves(n):
        kind, number = outgoing[n]
        if kind == "level":
            return None
        return lane_used(kind, number, heavy_wraps if kind == "heavy" else light_wraps)

    def spill_copy(n, stage):
        return remote(
            spill_out.at[n],
            spill_in.at[stage, n],
            spill_send.at[stage, n],
            spill_recv.at[stage, n],
            across,
        )

    def lane_copy(n, stage):
        row = index_of[outgoing[n]]
        return remote(
            lanes.at[n],
            arrived.at[stage, row, core],
            send_sem.at[stage, len(direct) + n, 0],
            recv_sem.at[stage, row, core],
            {"level": across, "heavy": heavy_to, "light": light_to}[outgoing[n][0]],
        )

    def mate_copy(row, stage):
        return remote(
            arrived.at[stage, row, core],
            arrived.at[stage, row, core],
            send_sem.at[stage, len(direct) + row, 1],
            recv_sem.at[stage, row, core],
            mate,
        )

    def cross_copy(row, stage):
        landing = index_of[("cross", rows[row][1])]
        return remote(
            arrived.at[stage, row, core],
            arrived.at[stage, landing, core],
            send_sem.at[stage, len(direct) + row, 2],
            recv_sem.at[stage, landing, core],
            across,
        )

    def share_copies(source, stage):
        return [
            remote(source.at[:, 1 - core], share_mine.at[stage], share_send.at[stage, 0], share_recv.at[stage, 0], mate),
            remote(source.at[:, core], share_other.at[stage], share_send.at[stage, 1], share_recv.at[stage, 1], mate),
        ]

    def wait_part(row, part, stage):
        remote(
            arrived.at[stage, row, part],
            arrived.at[stage, row, part],
            send_sem.at[stage, 0, 0],
            recv_sem.at[stage, row, part],
            mate,
        ).wait_recv()

    def hand_on(row, stage):
        kind, number = rows[row]
        wait_part(row, core, stage)
        mate_copy(row, stage).start()
        if kind == "heavy" and number < e_lanes:
            cross_copy(row, stage).start()

    def products(value, left, right):
        re_high, re_low = split(value[0])
        im_high, im_low = split(value[1])
        column = jnp.concatenate(
            [
                jnp.concatenate([re_high, re_low, re_high], axis=0),
                jnp.concatenate([im_high, im_low, im_high], axis=0),
            ],
            axis=1,
        )
        row = jnp.concatenate(
            [
                jnp.concatenate([re_high, re_low, re_high], axis=1),
                jnp.concatenate([im_high, im_low, im_high], axis=1),
            ],
            axis=0,
        )
        p = jnp.dot(left, column, preferred_element_type=F32)
        r = jnp.dot(row, right, preferred_element_type=F32)
        return p[:, :order], p[:, order:], r[:order], r[order:]

    def add_row(code, value, scale, stage):
        weight, target, mode, occ = code & 1, get(TARGET, code), get(MODE, code), get(OCC, code)
        lower = get(FLAG, code) == 1
        a = jnp.where(lower, F32(1.0), bath_ref[0, mode])
        b = jnp.where(lower, F32(0.0), bath_ref[1, mode])
        p_re, p_im, r_re, r_im = products(value, op_left[mode], op_right[mode])
        root = jnp.sqrt(jnp.full((1, order), occ, I32).astype(F32)) * weight.astype(F32) * scale
        ca = root * a
        cb = root * b
        term_ref[0] = ca * (p_im - r_im) + cb * (p_re + r_re)
        term_ref[1] = cb * (p_im + r_im) - ca * (p_re - r_re)

        def add_to(acc):
            def add(s, carry):
                chosen = jnp.where(target == s, F32(1.0), F32(0.0))
                acc[s] = acc[s] + chosen * term_ref[...]
                return carry

            lax.fori_loop(0, mats, add, 0)

        pl.when(stage == 0)(functools.partial(add_to, state.at[1]))
        pl.when(stage == 1)(functools.partial(add_to, out_ref))

    def prepare_operators():
        loads[1].wait()
        loads[2].wait()

        def prepare(k, carry):
            high, low = split(coup_ref[k])
            op_left[k] = jnp.concatenate([high, high, low], axis=1)
            op_right[k] = jnp.concatenate([high, high, low], axis=0)
            return carry

        lax.fori_loop(0, modes, prepare, 0)
        high, low = split(ham_ref[...])
        op_left[modes] = jnp.concatenate([high, high, low], axis=1)
        op_right[modes] = jnp.concatenate([high, high, low], axis=0)

    half_square = F32(0.5 * STEP * STEP)

    def stage_rows(stage, carry):
        source = state.at[stage]
        scale = jnp.where(stage == 0, F32(1.0), half_square)
        shares = share_copies(source, stage)

        for n in range(len(direct)):
            packed[n] = source[match_ref[direct[n], 0]]
            if n > 0:
                direct_copy(n - 1, stage, 0).start()
            if n == 1:
                shares[0].start()
        direct_copy(len(direct) - 1, stage, 0).start()
        shares[1].start()

        @pl.when(stage == 0)
        def _():
            prepare_operators()

        def own(n, carry):
            value = source[n]
            p_re, p_im, r_re, r_im = products(value, op_left[modes], op_right[modes])
            slope_re = (p_im - r_im) - damp_ref[n] * value[0]
            slope_im = (r_re - p_re) - damp_ref[n] * value[1]

            @pl.when(stage == 0)
            def _():
                state[1, n, 0] = slope_re
                state[1, n, 1] = slope_im

            @pl.when(stage == 1)
            def _():
                out_ref[n, 0] = state[0, n, 0] + F32(STEP) * value[0] + half_square * slope_re
                out_ref[n, 1] = state[0, n, 1] + F32(STEP) * value[1] + half_square * slope_im

            return carry

        lax.fori_loop(0, mats // 2, own, 0)

        shares[0].wait_recv()
        chip, other = me // 2, across // 2

        def chosen(code):
            slot = get(SLOT, code)
            return jnp.where(get(CORE, code) == core, source[slot, core], share_mine[stage, slot])

        for n in range(spills):
            spill_out[n] = chosen(spill_code(chip, heavy_wraps, n))
            if n > 0:
                spill_copy(n - 1, stage).start()

        def is_late(n):
            return outgoing[n][0] == "light" and outgoing[n][1] >= first_late

        early = [n for n in range(len(outgoing)) if not is_late(n)]
        late = [n for n in range(len(outgoing)) if is_late(n)]
        for turn, n in enumerate(early):
            kind, number = outgoing[n]
            if kind == "level":
                code = level_ref[chip * WIDTH + number]
            elif kind == "heavy":
                code = heavy_code(chip, heavy_wraps, number)
            else:
                code = light_code(chip, other, light_wraps, number)[0]
            lanes[n] = chosen(code)
            if turn > 0:
                before = early[turn - 1]
                when(leaves(before))(lane_copy(before, stage).start)
            else:
                if spills:
                    spill_copy(spills - 1, stage).start()
                direct_copy(len(direct) - 1, stage, 1).start()
        when(leaves(early[-1]))(lane_copy(early[-1], stage).start)

        lax.fori_loop(mats // 2, mats, own, 0)
        shares[1].wait_recv()

        def near_row(i, carry):
            code = fact[near + i]
            slot = get(SLOT, code)
            my_part = share_mine[stage, slot]
            other_part = share_other[stage, slot]
            is_real = core == 0
            value = (jnp.where(is_real, my_part, other_part), jnp.where(is_real, other_part, my_part))
            add_row(code, value, scale, stage)
            return carry

        lax.fori_loop(0, 2, near_row, 0)

        for n in range(spills):
            spill_copy(n, stage).wait_recv()
        for n in late:
            code, taken, inside = light_code(chip, other, light_wraps, outgoing[n][1])
            value = chosen(code)
            if spills:
                value = jnp.where(taken, spill_in[stage, inside], value)
            lanes[n] = value
        for n in late:
            when(leaves(n))(lane_copy(n, stage).start)
        for n in range(len(direct) - 1):
            direct_copy(n, stage, 1).start()

        def row_step(i, carry):
            there = i >= 0
            is_lane = i < 0
            for row in lane_rows:
                used = lands(row)
                now = i == max(row - 2, 0)
                when(now if used is None else now & used)(functools.partial(hand_on, row, stage))
                is_lane = is_lane | (i == row)
                if used is not None:
                    there = there & ((i != row) | used)

            @pl.when(there)
            def _():
                wait_part(i, 1 - core, stage)

                @pl.when(jnp.logical_not(is_lane))
                def _():
                    wait_part(i, core, stage)

                add_row(fact[i], arrived[stage, i], scale, stage)

            return carry

        lax.fori_loop(0, len(rows), row_step, 0)

        for share in shares:
            share.wait_send()
        for n in range(spills):
            spill_copy(n, stage).wait_send()
        for n in range(len(direct)):
            for part in range(2):
                direct_copy(n, stage, part).wait_send()
        for n in range(len(outgoing)):
            when(leaves(n))(lane_copy(n, stage).wait_send)
        for row in lane_rows:
            kind, number = rows[row]

            def sent():
                mate_copy(row, stage).wait_send()
                if kind == "heavy" and number < e_lanes:
                    cross_copy(row, stage).wait_send()

            when(lands(row))(sent)
        return carry

    loads[0].wait()
    lax.fori_loop(0, 2, stage_rows, 0)


def body(tier_size, rho, hamiltonian, couplings, bath_coef, damping, match_edges, left_rows, left_count):
    mats, _, order, _ = rho.shape
    modes = couplings.shape[0]
    table = match_edges.reshape(-1, match_edges.shape[-1])
    colours = table.shape[0]
    vmem = pl.BlockSpec(memory_space=pltpu.VMEM)
    hbm = pl.BlockSpec(memory_space=pl.ANY)
    smem = pl.BlockSpec(memory_space=pltpu.SMEM)

    pair, heavy, light, level, count, pick = pl.pallas_call(
        functools.partial(plan_kernel, tier_size, mats),
        out_shape=[
            jax.ShapeDtypeStruct((tier_size * 2 * REACH + 1,), I32),
            jax.ShapeDtypeStruct((tier_size // 2 * WIDTH,), I32),
            jax.ShapeDtypeStruct((tier_size // 2 * WIDTH,), I32),
            jax.ShapeDtypeStruct((tier_size // 2 * WIDTH,), I32),
            jax.ShapeDtypeStruct((tier_size // 2,), I32),
            jax.ShapeDtypeStruct((1,), I32),
        ],
        in_specs=[smem, smem],
        out_specs=[smem] * 6,
    )(left_rows.transpose(2, 1, 0), left_count)

    def step(number, variant):
        order_of_rows = row_order(variant, colours)
        rows = len(order_of_rows)
        lanes = sum(kind in ("level", "heavy", "light") for kind, _ in order_of_rows)
        direct = colours - 1
        spills = max(variant[4], 1)
        return pl.pallas_call(
            functools.partial(kernel, tier_size, colours, variant),
            out_shape=pltpu.VMEM(rho.shape, F32),
            in_specs=[hbm, hbm, hbm] + [smem] * 8,
            out_specs=vmem,
            scratch_shapes=[
                pltpu.VMEM((2,) + rho.shape, F32),
                pltpu.VMEM(hamiltonian.shape, F32),
                pltpu.VMEM(couplings.shape, F32),
                pltpu.SemaphoreType.DMA((3,)),
                pltpu.VMEM((2, order, order), F32),
                pltpu.VMEM((2, mats, order, order), F32),
                pltpu.VMEM((2, mats, order, order), F32),
                pltpu.VMEM((direct, 2, order, order), F32),
                pltpu.VMEM((lanes, order, order), F32),
                pltpu.VMEM((spills, order, order), F32),
                pltpu.VMEM((2, spills, order, order), F32),
                pltpu.VMEM((2, rows, 2, order, order), F32),
                pltpu.VMEM((modes + 1, order, 3 * order), BF16),
                pltpu.VMEM((modes + 1, 3 * order, order), BF16),
                pltpu.SMEM((rows + 2,), I32),
                pltpu.SemaphoreType.DMA((2, 2)),
                pltpu.SemaphoreType.DMA((2, 2)),
                pltpu.SemaphoreType.DMA((2, spills)),
                pltpu.SemaphoreType.DMA((2, spills)),
                pltpu.SemaphoreType.DMA((2, direct + rows, 3)),
                pltpu.SemaphoreType.DMA((2, rows, 2)),
            ],
            compiler_params=pltpu.CompilerParams(
                collective_id=number, has_side_effects=True, vmem_limit_bytes=58 * 1024 * 1024
            ),
        )

    return lax.switch(
        pick[0],
        [step(i, variant) for i, variant in enumerate(VARIANTS)],
        rho,
        hamiltonian,
        couplings,
        bath_coef.T,
        damping,
        table,
        pair,
        heavy,
        light,
        level,
        count,
    )


def solution(mesh):
    placed = (
        P(("groups", "tier"), None, None, None),
        P(),
        P(),
        P("groups", None),
        P(("groups", "tier")),
        P("tier", None, None, None),
        P(),
        P(),
    )
    return jax.shard_map(
        functools.partial(body, mesh.shape["tier"]),
        mesh=mesh,
        in_specs=placed,
        out_specs=P(("groups", "tier"), None, None, None),
        check_vma=False,
    )
```
